512 devices in a mesh: blk: 128 (over y, z, core), pitch: 4 (over x).
Axes of the slice: x: 4, y: 8, z: 8, core: 2. Of those that a mesh axis runs over, the one named last changes fastest.
Arguments:
- states: float32 [2, 5, 1024, 32, 128], P(None, None, 'blk', 'pitch'), may hold values from -6 to 6
- time_steps: float32 [2, 1024, 32, 128], P(None, 'blk', 'pitch'), may hold values from 0.05 to 0.4
- speeds: float32 [2, 5, 3], replicated, may hold values from 0.2 to 0.7
- band_src: int32 [2, 1024, 3], P(None, 'blk'), may hold values from 0 to 1023, as said below
- band_frac: int32 [2, 1024, 3], P(None, 'blk'), may hold values from 0 to 65536, as said below
Outputs:
- states_out: float32 [2, 5, 1024, 32, 128], P(None, None, 'blk', 'pitch')
- arrivals: float32 [2, 1024, 480], P(None, 'blk', 'pitch')
The draws below stay inside these ranges and needn't reach their ends.
Inputs may be any that keep to these rules, and one draw needn't show every extreme that they name: `band_src`: row j of either table names, in its 3 slots in some order, rows j - 1, j, j + 1 of the other blade row where they exist and j itself otherwise; every named row lies within one row of j. `band_frac`: A slot naming a row that does not intersect the receiving row has fraction 0; a row's fractions sum to at most 65536.
All inputs are finite; a program needn't handle non-finite values.
Results may differ from the reference program's by a relative error of at most 0.000075.
Values sent between devices are 32-bit elements; how exact they have to be, the bound alone decides.
A program may use at most 64 MiB of HBM per device.

```python
import math
import jax
import jax.numpy as jnp
import numpy as np
from jax import lax

NV = 5
NH = 48
AX = 128
RAD = 1024
PIT = 32
NCOEF = 480


slot_orders = np.array([[0, 1, 2], [0, 2, 1], [1, 0, 2], [1, 2, 0], [2, 0, 1], [2, 1, 0]], dtype=np.int32)


def band_tables(key):
    inner_count = RAD - 1
    magnitude = jax.random.randint(jax.random.fold_in(key, 11), (inner_count,), 8, 25).astype(jnp.int32)
    flips = jax.random.randint(jax.random.fold_in(key, 13), (inner_count,), 0, 2).astype(jnp.int32)
    shifts = magnitude * (2 * flips - 1)
    edge_shift = jnp.concatenate([jnp.zeros((1,), jnp.int32), shifts, jnp.zeros((1,), jnp.int32)])
    vane_edges = (64 * jnp.arange(RAD + 1, dtype=jnp.int32) + edge_shift).astype(jnp.int32)
    vane_widths = (vane_edges[1:] - vane_edges[:-1]).astype(jnp.int32)
    row_ids = jnp.arange(RAD, dtype=jnp.int32)
    offsets = jnp.array([-1, 0, 1], dtype=jnp.int32)
    candidate = row_ids[:, None] + offsets[None, :]
    usable = (candidate >= 0) & (candidate < RAD)
    clipped = jnp.clip(candidate, 0, RAD - 1)
    lower_vane = jnp.maximum(vane_edges[:-1][:, None], clipped * 64)
    upper_vane = jnp.minimum(vane_edges[1:][:, None], clipped * 64 + 64)
    intersection_vane = jnp.where(usable, jnp.maximum(upper_vane - lower_vane, 0), 0)
    share_vane = intersection_vane * 65536 // vane_widths[:, None]
    lower_fan = jnp.maximum(row_ids[:, None] * 64, vane_edges[clipped])
    upper_fan = jnp.minimum(row_ids[:, None] * 64 + 64, vane_edges[clipped + 1])
    share_fan = jnp.where(usable, jnp.maximum(upper_fan - lower_fan, 0), 0) * 1024
    sources = jnp.where(usable, clipped, row_ids[:, None])
    both_src = jnp.stack([sources, sources]).astype(jnp.int32)
    both_share = jnp.stack([share_fan, share_vane]).astype(jnp.int32)
    choose = jax.random.randint(jax.random.fold_in(key, 12), (2, RAD), 0, 6)
    arrange = jnp.asarray(slot_orders)[choose]
    return (jnp.take_along_axis(both_src, arrange, 2).astype(jnp.int32), jnp.take_along_axis(both_share, arrange, 2).astype(jnp.int32))


def draw_band_src(key, part):
    return band_tables(key)[0]


def draw_band_frac(key, part):
    return band_tables(key)[1]


def block_levels(rng, shape, shards, low, largest):
    loudness = 1.0
    for position, blocks in shards:
        steps = jax.random.uniform(jax.random.fold_in(jax.random.fold_in(rng, 6), position), (blocks,), jnp.float32, low / len(shards), largest / len(shards))
        loudness = loudness * jnp.repeat(jnp.exp(steps), shape[position] // blocks).reshape((-1,) + (1,) * (len(shape) - 1 - position))
    return loudness


def noise(stream_key, dims, spread, most, split=(), kind=jnp.bfloat16):
    loudness = block_levels(stream_key, dims, split, -0.22, 0.18) if split else 1.0
    entries = jax.random.normal(stream_key, dims, jnp.float32) * spread * loudness
    return jnp.minimum(jnp.maximum(entries, -most), most).astype(kind)


def setup_inputs(seed: int = 0) -> dict:
    arg_keys = jax.random.split(jax.random.key(seed), 6)
    return {
        "states": noise(arg_keys[0], (2, NV, RAD, PIT, AX), 1.0, 6.0, ((2, 128), (3, 4)), jnp.float32),
        "time_steps": jnp.clip(jnp.exp(math.log(0.4) - 2.0794415 * jax.random.uniform(arg_keys[1], (2, RAD, PIT, AX), jnp.float32) ** block_levels(arg_keys[1], (2, RAD, PIT, AX), ((1, 128), (2, 4)), -0.2, 0.2)), 0.05, 0.4),
        "speeds": jnp.clip(jax.random.uniform(arg_keys[2], (2, NV, 3), jnp.float32, 0.2, 0.7), 0.2, 0.7),
        "band_src": draw_band_src(jax.random.fold_in(arg_keys[5], 71), 0),
        "band_frac": draw_band_frac(jax.random.fold_in(arg_keys[5], 71), 0),
    }


viscosity = 0.15
section_weights = (1.0 / 3.0, 0.5, 1.0)


def harmonic_table(places, period, count):
    orders = jnp.arange(count, dtype=jnp.int32)
    cos_phase = ((places[:, None] * orders[None, :]) % period).astype(jnp.float32)
    sin_phase = ((places[:, None] * (orders[None, :] + 1)) % period).astype(jnp.float32)
    factor = jnp.where(orders == 0, 1.0, 2.0).astype(jnp.float32) / period
    cos_cols = jnp.cos(2.0 * math.pi * cos_phase / period) * factor[None, :]
    sin_cols = jnp.sin(2.0 * math.pi * sin_phase / period) * (2.0 / period)
    return jnp.concatenate([cos_cols, sin_cols], 1).astype(jnp.float32)


def residual(extended, speeds):
    centre = extended[:, :, 1:-1, 1:-1, :]
    zero_face = jnp.zeros_like(centre[..., :1])
    axial_low = jnp.concatenate([zero_face, centre[..., :-1]], 4)
    axial_high = jnp.concatenate([centre[..., 1:], zero_face], 4)
    radial_low = extended[:, :, :-2, 1:-1, :]
    radial_high = extended[:, :, 2:, 1:-1, :]
    pitch_low = extended[:, :, 1:-1, :-2, :]
    pitch_high = extended[:, :, 1:-1, 2:, :]
    speed_axial = speeds[:, :, 0][:, :, None, None, None]
    speed_radial = speeds[:, :, 1][:, :, None, None, None]
    speed_pitch = speeds[:, :, 2][:, :, None, None, None]
    neighbours = axial_low + axial_high + radial_low + radial_high + pitch_low + pitch_high
    return (-speed_axial * (centre - axial_low) - speed_radial * (centre - radial_low)
            - speed_pitch * (centre - pitch_low) + viscosity * (neighbours - 6.0 * centre))


def extend_field(field):
    wrapped = jnp.concatenate([field[:, :, :, -1:], field, field[:, :, :, :1]], 3)
    return jnp.pad(wrapped, ((0, 0), (0, 0), (1, 1), (0, 0), (0, 0)))


def pick_rows(source_table, indices):
    return source_table[indices]


def reference(states, time_steps, speeds, band_src, band_frac):
    field = states
    for weight_of in section_weights:
        field = states + weight_of * time_steps[:, None] * residual(extend_field(field), speeds)
    planes = jnp.stack([field[0, :, :, :, AX - 1], field[1, :, :, :, 0]])
    table = harmonic_table(jnp.arange(PIT, dtype=jnp.int32), PIT, NH)
    coef_all = jnp.einsum('wvrp,pm->wrvm', planes, table, precision=lax.Precision.HIGHEST)
    coef_all = coef_all.reshape(2, RAD, NCOEF)
    picked = jax.vmap(pick_rows)(coef_all[::-1], band_src)
    weights = band_frac.astype(jnp.float32) * (1.0 / 65536.0)
    arrivals = jnp.sum(weights[..., None] * picked, axis=2)
    return field, arrivals
```

```python
import functools

import jax
import jax.numpy as jnp
import numpy as np
from jax import lax
from jax.experimental import pallas as pl
from jax.experimental.pallas import tpu as pltpu
from jax.sharding import PartitionSpec as P

NH = 48
NV = 5
WV = 2 * NV
ROWS = 8
NU = 0.15
section_weights = (1.0 / 3.0, 0.5, 1.0)
MESH = pl.DeviceIdType.MESH
HIGHEST = lax.Precision.HIGHEST
PEERS = [(db, dx) for db in (0, -1, 1) for dx in (0, 1, 3, 2) if (db, dx) != (0, 0)]


def harmonic_tables(slabs, slab):
    period = slabs * slab
    places = np.arange(period)[:, None]
    orders = np.arange(NH)[None, :]
    factor = np.where(orders == 0, 1.0, 2.0) / period
    cos_cols = np.cos(2.0 * np.pi * (places * orders % period) / period) * factor
    sin_cols = np.sin(2.0 * np.pi * (places * (orders + 1) % period) / period) * (2.0 / period)
    table = np.concatenate([cos_cols, sin_cols], 1)
    total = NV * 2 * NH
    chunk = total // slabs
    full = np.zeros((NV, period, total))
    for v in range(NV):
        full[v, :, v * 2 * NH:(v + 1) * 2 * NH] = table
    full = full.reshape(NV, slabs, slab, slabs, chunk).transpose(3, 1, 0, 2, 4)
    out = np.zeros((slabs, slabs, NV, slab, 128), np.float32)
    out[..., :chunk] = full
    return out


def kernel(blocks, slabs, speeds, states_hbm, steps_hbm, table_hbm, src_ref, frac_ref,
           out_ref, arr_ref,
           q0, dt, table, partial, field, send, halo, inter, inter_b, inter_c,
           load_sem, send_sem, recv_sem, isend_sem, irecv_sem):
    b = lax.axis_index("blk")
    x = lax.axis_index("pitch")

    def device(db, dx):
        return {"blk": lax.rem(b + db + blocks, blocks), "pitch": lax.rem(x + dx + slabs, slabs)}

    loads = [
        pltpu.make_async_copy(states_hbm, q0, load_sem.at[0]),
        pltpu.make_async_copy(steps_hbm, dt, load_sem.at[1]),
        pltpu.make_async_copy(table_hbm.at[x], table, load_sem.at[2]),
    ]
    for load in loads:
        load.start()
    barrier = pltpu.get_barrier_semaphore()
    for db, dx in PEERS:
        pl.semaphore_signal(barrier, inc=1, device_id=device(db, dx), device_id_type=MESH)

    lane = lax.broadcasted_iota(jnp.int32, (8, 128), 1)
    sub = lax.broadcasted_iota(jnp.int32, (8, 128), 0)
    low_edge = jnp.where(b == 0, 0.0, 1.0)
    high_edge = jnp.where(b == blocks - 1, 0.0, 1.0)

    def pack(source, stage):
        def body(i, carry):
            base = pl.multiple_of(i * 64, 64)
            send[stage, 0, i] = source[pl.ds(base + 7, 8, stride=8), :]
            send[stage, 1, i] = source[pl.ds(base, 8, stride=8), :]
            send[stage, 2, i] = source[pl.ds(base + 56, 8), :]
            send[stage, 3, i] = source[pl.ds(base, 8), :]
            return carry
        lax.fori_loop(0, WV, body, 0)

    def exchange(stage):
        copies = []
        for d, (db, dx) in enumerate(((0, 1), (0, -1), (1, 0), (-1, 0))):
            copies.append(pltpu.make_async_remote_copy(
                src_ref=send.at[stage, d], dst_ref=halo.at[stage, d],
                send_sem=send_sem.at[stage, d], recv_sem=recv_sem.at[stage, d],
                device_id=device(db, dx), device_id_type=MESH))
        return copies

    loads[0].wait()
    loads[1].wait()
    pack(q0, 0)
    chosen = []
    for w in range(2):
        first = 124 if w == 0 else -4
        pick = jnp.where((sub // 4 == w) & (lane == sub + first), 1.0, 0.0)
        cells = jnp.concatenate([q0[w * 320:(w + 1) * 320, :], dt[w * 64:(w + 1) * 64, :]], 0)
        chosen.append(lax.dot_general(pick, cells, (((1,), (1,)), ((), ())),
                                      precision=HIGHEST, preferred_element_type=jnp.float32))
    packet = chosen[0] + chosen[1]
    for j in range(3):
        inter[1, x, j] = packet[:, j * 128:(j + 1) * 128]

    pl.semaphore_wait(barrier, len(PEERS))
    stages = [exchange(stage) for stage in range(3)]
    for copy in stages[0]:
        copy.start()
    gathers = []
    for k, (db, dx) in enumerate(PEERS):
        gathers.append(pltpu.make_async_remote_copy(
            src_ref=inter.at[1, x], dst_ref=inter.at[1 - db, x],
            send_sem=isend_sem.at[k], recv_sem=irecv_sem.at[k],
            device_id=device(db, dx), device_id_type=MESH))
    for copy in gathers:
        copy.start()

    def inner(source, weight):
        def body(i, carry):
            base = pl.multiple_of(i * 64, 64)
            dbase = pl.multiple_of((i // NV) * 64, 64)
            a0, a1, a2 = speeds[i * 3], speeds[i * 3 + 1], speeds[i * 3 + 2]
            centre = -(a0 + a1 + a2) - 6.0 * NU
            axial_low = jnp.where(lane == 0, 0.0, a0 + NU)
            axial_high = jnp.where(lane == 127, 0.0, NU)
            pitch_low = jnp.where(sub == 0, 0.0, a2 + NU)
            pitch_high = jnp.where(sub == 7, 0.0, NU)
            rows = [source[pl.ds(base + r * 8, 8), :] for r in range(ROWS)]
            for r in range(ROWS):
                q = rows[r]
                total = centre * q
                total += axial_low * pltpu.roll(q, 1, 1)
                total += axial_high * pltpu.roll(q, 127, 1)
                total += pitch_low * pltpu.roll(q, 1, 0)
                total += pitch_high * pltpu.roll(q, 7, 0)
                if r > 0:
                    total += (a1 + NU) * rows[r - 1]
                if r < ROWS - 1:
                    total += NU * rows[r + 1]
                step = weight * dt[pl.ds(dbase + r * 8, 8), :]
                partial[pl.ds(base + r * 8, 8), :] = q0[pl.ds(base + r * 8, 8), :] + step * total
            return carry
        lax.fori_loop(0, WV, body, 0)

    def outer(stage, target, weight):
        def body(i, carry):
            base = pl.multiple_of(i * 64, 64)
            dbase = pl.multiple_of((i // NV) * 64, 64)
            a1, a2 = speeds[i * 3 + 1], speeds[i * 3 + 2]
            pitch_low = jnp.where(sub == 0, a2 + NU, 0.0)
            pitch_high = jnp.where(sub == 7, NU, 0.0)
            for r in range(ROWS):
                total = pitch_low * halo[stage, 0, i, pl.ds(r, 1), :]
                total += pitch_high * halo[stage, 1, i, pl.ds(r, 1), :]
                if r == 0:
                    total += (low_edge * (a1 + NU)) * halo[stage, 2, i]
                if r == ROWS - 1:
                    total += (high_edge * NU) * halo[stage, 3, i]
                step = weight * dt[pl.ds(dbase + r * 8, 8), :]
                target[pl.ds(base + r * 8, 8), :] = (
                    partial[pl.ds(base + r * 8, 8), :] + step * total)
            return carry
        lax.fori_loop(0, WV, body, 0)

    def speed_lanes(k, j):
        def of(w, v):
            return speeds[(w * NV + v) * 3 + k] if v < NV else 0.0
        return jnp.where(sub < 4,
                         jnp.where(lane < 64, of(0, 2 * j), of(0, 2 * j + 1)),
                         jnp.where(lane < 64, of(1, 2 * j), of(1, 2 * j + 1)))

    def interface_coefs():
        coefs = []
        for j in range(3):
            nu = NU if j < 2 else jnp.where(lane < 64, NU, 0.0)
            a0, a1, a2 = (speed_lanes(k, j) for k in range(3))
            coefs.append((-(a0 + a1 + a2) - 6.0 * nu,
                          jnp.where(sub == 4, 0.0, a0 + nu), jnp.where(sub == 3, 0.0, nu),
                          a1 + nu, nu, a2 + nu, nu))
        return coefs

    cell = lax.rem(lane, 8)
    row = lax.rem(lane, 64) // 8

    def interface_section(source, weight, coefs, s):
        before = lax.rem(s + slabs - 1, slabs)
        after = lax.rem(s + 1, slabs)
        result = []
        for d in range(3):
            last = inter[d, s, 2]
            step = weight * jnp.where(lane < 64, pltpu.roll(last, 64, 1), last)
            parts = []
            for j in range(3):
                c, xl, xh, rl, rh, pl_, ph = coefs[j]
                q = source[d, s, j]
                total = c * q + xl * pltpu.roll(q, 1, 0) + xh * pltpu.roll(q, 7, 0)
                total += pl_ * jnp.where(cell == 0, pltpu.roll(source[d, before, j], 121, 1),
                                         pltpu.roll(q, 1, 1))
                total += ph * jnp.where(cell == 7, pltpu.roll(source[d, after, j], 7, 1),
                                        pltpu.roll(q, 127, 1))
                low = pltpu.roll(q, 8, 1)
                if d > 0:
                    low = jnp.where(row == 0, pltpu.roll(source[d - 1, s, j], 72, 1), low)
                high = pltpu.roll(q, 120, 1)
                if d < 2:
                    high = jnp.where(row == 7, pltpu.roll(source[d + 1, s, j], 56, 1), high)
                total += rl * low + rh * high
                parts.append(inter[d, s, j] + step * total)
            result.append(parts)
        return result

    def interface_step(source, target, weight):
        def body(s, carry):
            coefs = interface_coefs()
            result = interface_section(source, weight, coefs, s)
            for d in range(3):
                for j in range(3):
                    target[d, s, j] = result[d][j]
            return carry
        lax.fori_loop(0, slabs, body, 0)

    def interface_last(source, weight):
        shares = []
        for w in range(2):
            per_block = []
            for d in range(3):
                place = (b + d - 1) * ROWS + row
                share = jnp.zeros((8, 128), jnp.float32)
                for slot in range(3):
                    share += jnp.where(src_ref[w, :, slot:slot + 1] == place,
                                       frac_ref[w, :, slot:slot + 1].astype(jnp.float32)
                                       * (1.0 / 65536.0), 0.0)
                per_block.append(share)
            shares.append(per_block)

        def body(s, total):
            coefs = interface_coefs()
            result = interface_section(source, weight, coefs, s)
            sides = []
            for w in range(2):
                at = 4 if w == 0 else 3
                columns = []
                for j in range(3):
                    columns.append(sum(jnp.broadcast_to(result[d][j][at:at + 1, :], (8, 128))
                                       * shares[w][d] for d in range(3)))
                sides.append(jnp.concatenate(columns, 1))
            lhs = jnp.concatenate(sides, 0)
            waves = []
            for v in range(NV):
                waves += [table[s, v]] * ROWS
            waves.append(jnp.zeros((64, 128), jnp.float32))
            rhs = jnp.concatenate(waves, 0)
            return total + jnp.dot(lhs, rhs, precision=HIGHEST,
                                   preferred_element_type=jnp.float32)
        total = lax.fori_loop(0, slabs, body, jnp.zeros((16, 128), jnp.float32))
        columns = arr_ref.shape[2]
        arr_ref[0] = total[0:8, 0:columns]
        arr_ref[1] = total[8:16, 0:columns]

    w1, w2, w3 = section_weights
    inner(q0, w1)
    for copy in stages[0]:
        copy.wait_recv()
    outer(0, field, w1)
    pack(field, 1)
    for copy in stages[1]:
        copy.start()

    inner(field, w2)
    for copy in gathers:
        copy.wait_send()
    for copy in gathers:
        copy.wait_recv()

    def edges(s, carry):
        for j in range(3):
            inter[0, s, j] = inter[0, s, j] * low_edge
            inter[2, s, j] = inter[2, s, j] * high_edge
        return carry
    lax.fori_loop(0, slabs, edges, 0)
    interface_step(inter, inter_b, w1)
    for copy in stages[1]:
        copy.wait_recv()
    outer(1, field, w2)
    pack(field, 2)
    for copy in stages[2]:
        copy.start()

    inner(field, w3)
    interface_step(inter_b, inter_c, w2)
    loads[2].wait()
    interface_last(inter_c, w3)
    for copy in stages[2]:
        copy.wait_recv()
    outer(2, out_ref, w3)
    for stage in stages:
        for copy in stage:
            copy.wait_send()


def shards(tables, states, time_steps, speeds, band_src, band_frac):
    blocks = lax.axis_size("blk")
    slabs = lax.axis_size("pitch")
    any_space = pl.BlockSpec(memory_space=pl.ANY)
    vmem = pl.BlockSpec(memory_space=pltpu.VMEM)
    cells = WV * ROWS * 8
    columns = NV * 2 * NH // slabs
    field, arrivals = pl.pallas_call(
        functools.partial(kernel, blocks, slabs),
        out_shape=(jax.ShapeDtypeStruct((cells, 128), jnp.float32),
                   jax.ShapeDtypeStruct((2, ROWS, columns), jnp.float32)),
        in_specs=[pl.BlockSpec(memory_space=pltpu.SMEM), any_space, any_space, any_space,
                  vmem, vmem],
        out_specs=(vmem, vmem),
        scratch_shapes=[
            pltpu.VMEM((cells, 128), jnp.float32),
            pltpu.VMEM((128, 128), jnp.float32),
            pltpu.VMEM((slabs, NV, 8, 128), jnp.float32),
            pltpu.VMEM((cells, 128), jnp.float32),
            pltpu.VMEM((cells, 128), jnp.float32),
            pltpu.VMEM((3, 4, WV, 8, 128), jnp.float32),
            pltpu.VMEM((3, 4, WV, 8, 128), jnp.float32),
            pltpu.VMEM((3, slabs, 3, 8, 128), jnp.float32),
            pltpu.VMEM((3, slabs, 3, 8, 128), jnp.float32),
            pltpu.VMEM((3, slabs, 3, 8, 128), jnp.float32),
            pltpu.SemaphoreType.DMA((3,)),
            pltpu.SemaphoreType.DMA((3, 4)),
            pltpu.SemaphoreType.DMA((3, 4)),
            pltpu.SemaphoreType.DMA((len(PEERS),)),
            pltpu.SemaphoreType.DMA((len(PEERS),)),
        ],
        compiler_params=pltpu.CompilerParams(collective_id=0, has_side_effects=True),
        name="window",
    )(speeds.reshape(-1), states.reshape(cells, 128), time_steps.reshape(128, 128),
      jnp.asarray(tables), band_src, band_frac)
    return field.reshape(states.shape), arrivals


def solution(mesh):
    tables = harmonic_tables(mesh.shape["pitch"], 8)
    return jax.shard_map(
        functools.partial(shards, tables),
        mesh=mesh,
        in_specs=(
            P(None, None, "blk", "pitch", None),
            P(None, "blk", "pitch", None),
            P(),
            P(None, "blk", None),
            P(None, "blk", None),
        ),
        out_specs=(P(None, None, "blk", "pitch", None), P(None, "blk", "pitch")),
        check_vma=False,
    )
```

```python
import functools

import jax
import jax.numpy as jnp
import numpy as np
from jax import lax
from jax.experimental import pallas as pl
from jax.experimental.pallas import tpu as pltpu
from jax.sharding import PartitionSpec as P

NH = 48
NV = 5
WV = 2 * NV
ROWS = 8
NU = 0.15
section_weights = (1.0 / 3.0, 0.5, 1.0)
MESH = pl.DeviceIdType.MESH
HIGHEST = lax.Precision.HIGHEST
PEERS = [(db, dx) for db in (0, -1, 1) for dx in (0, 1, 3, 2) if (db, dx) != (0, 0)]


def harmonic_tables(slabs, slab):
    period = slabs * slab
    places = np.arange(period)[:, None]
    orders = np.arange(NH)[None, :]
    factor = np.where(orders == 0, 1.0, 2.0) / period
    cos_cols = np.cos(2.0 * np.pi * (places * orders % period) / period) * factor
    sin_cols = np.sin(2.0 * np.pi * (places * (orders + 1) % period) / period) * (2.0 / period)
    table = np.concatenate([cos_cols, sin_cols], 1)
    total = NV * 2 * NH
    chunk = total // slabs
    full = np.zeros((NV, period, total))
    for v in range(NV):
        full[v, :, v * 2 * NH:(v + 1) * 2 * NH] = table
    full = full.reshape(NV, slabs, slab, slabs, chunk).transpose(3, 1, 0, 2, 4)
    out = np.zeros((slabs, slabs, NV, slab, 128), np.float32)
    out[..., :chunk] = full
    return out


def kernel(blocks, slabs, speeds_hbm, states_hbm, steps_hbm, table_hbm, src_hbm, frac_hbm,
           out_ref, arr_ref,
           speeds, src_ref, frac_ref, q0, dt, table, partial, field, send, halo, inter, inter_b, inter_c,
           load_sem, send_sem, recv_sem, isend_sem, irecv_sem):
    b = lax.axis_index("blk")
    x = lax.axis_index("pitch")

    def device(db, dx):
        return {"blk": lax.rem(b + db + blocks, blocks), "pitch": lax.rem(x + dx + slabs, slabs)}

    barrier = pltpu.get_barrier_semaphore()
    for db, dx in PEERS:
        pl.semaphore_signal(barrier, inc=1, device_id=device(db, dx), device_id_type=MESH)
    loads = [
        pltpu.make_async_copy(states_hbm, q0, load_sem.at[0]),
        pltpu.make_async_copy(steps_hbm, dt, load_sem.at[1]),
        pltpu.make_async_copy(table_hbm.at[x], table, load_sem.at[2]),
        pltpu.make_async_copy(speeds_hbm, speeds, load_sem.at[3]),
        pltpu.make_async_copy(src_hbm, src_ref, load_sem.at[4]),
        pltpu.make_async_copy(frac_hbm, frac_ref, load_sem.at[5]),
    ]
    for load in loads:
        load.start()

    lane = lax.broadcasted_iota(jnp.int32, (8, 128), 1)
    sub = lax.broadcasted_iota(jnp.int32, (8, 128), 0)
    low_edge = jnp.where(b == 0, 0.0, 1.0)
    high_edge = jnp.where(b == blocks - 1, 0.0, 1.0)

    def pack(source, stage):
        def body(i, carry):
            base = pl.multiple_of(i * 64, 64)
            send[stage, 0, i] = source[pl.ds(base + 7, 8, stride=8), :]
            send[stage, 1, i] = source[pl.ds(base, 8, stride=8), :]
            send[stage, 2, i] = source[pl.ds(base + 56, 8), :]
            send[stage, 3, i] = source[pl.ds(base, 8), :]
            return carry
        lax.fori_loop(0, WV, body, 0)

    def exchange(stage):
        copies = []
        for d, (db, dx) in enumerate(((0, 1), (0, -1), (1, 0), (-1, 0))):
            copies.append(pltpu.make_async_remote_copy(
                src_ref=send.at[stage, d], dst_ref=halo.at[stage, d],
                send_sem=send_sem.at[stage, d], recv_sem=recv_sem.at[stage, d],
                device_id=device(db, dx), device_id_type=MESH))
        return copies

    loads[0].wait()
    loads[1].wait()
    pack(q0, 0)
    chosen = []
    for w in range(2):
        first = 124 if w == 0 else -4
        pick = jnp.where((sub // 4 == w) & (lane == sub + first), 1.0, 0.0)
        cells = jnp.concatenate([q0[w * 320:(w + 1) * 320, :], dt[w * 64:(w + 1) * 64, :]], 0)
        chosen.append(lax.dot_general(pick, cells, (((1,), (1,)), ((), ())),
                                      precision=HIGHEST, preferred_element_type=jnp.float32))
    packet = chosen[0] + chosen[1]
    for j in range(3):
        inter[1, x, j] = packet[:, j * 128:(j + 1) * 128]

    pl.semaphore_wait(barrier, len(PEERS))
    stages = [exchange(stage) for stage in range(3)]
    for copy in stages[0]:
        copy.start()
    gathers = []
    for k, (db, dx) in enumerate(PEERS):
        gathers.append(pltpu.make_async_remote_copy(
            src_ref=inter.at[1, x], dst_ref=inter.at[1 - db, x],
            send_sem=isend_sem.at[k], recv_sem=irecv_sem.at[k],
            device_id=device(db, dx), device_id_type=MESH))
    for copy in gathers:
        copy.start()

    def inner(source, weight):
        def body(i, carry):
            base = pl.multiple_of(i * 64, 64)
            dbase = pl.multiple_of((i // NV) * 64, 64)
            a0, a1, a2 = (speeds[k, i // NV, lax.rem(i, NV)] for k in range(3))
            centre = -(a0 + a1 + a2) - 6.0 * NU
            axial_low = jnp.where(lane == 0, 0.0, a0 + NU)
            axial_high = jnp.where(lane == 127, 0.0, NU)
            pitch_low = jnp.where(sub == 0, 0.0, a2 + NU)
            pitch_high = jnp.where(sub == 7, 0.0, NU)
            rows = [source[pl.ds(base + r * 8, 8), :] for r in range(ROWS)]
            for r in range(ROWS):
                q = rows[r]
                total = centre * q
                total += axial_low * pltpu.roll(q, 1, 1)
                total += axial_high * pltpu.roll(q, 127, 1)
                total += pitch_low * pltpu.roll(q, 1, 0)
                total += pitch_high * pltpu.roll(q, 7, 0)
                if r > 0:
                    total += (a1 + NU) * rows[r - 1]
                if r < ROWS - 1:
                    total += NU * rows[r + 1]
                step = weight * dt[pl.ds(dbase + r * 8, 8), :]
                partial[pl.ds(base + r * 8, 8), :] = q0[pl.ds(base + r * 8, 8), :] + step * total
            return carry
        lax.fori_loop(0, WV, body, 0)

    def outer(stage, target, weight):
        def body(i, carry):
            base = pl.multiple_of(i * 64, 64)
            dbase = pl.multiple_of((i // NV) * 64, 64)
            a1, a2 = (speeds[k, i // NV, lax.rem(i, NV)] for k in range(1, 3))
            pitch_low = jnp.where(sub == 0, a2 + NU, 0.0)
            pitch_high = jnp.where(sub == 7, NU, 0.0)
            for r in range(ROWS):
                total = pitch_low * halo[stage, 0, i, pl.ds(r, 1), :]
                total += pitch_high * halo[stage, 1, i, pl.ds(r, 1), :]
                if r == 0:
                    total += (low_edge * (a1 + NU)) * halo[stage, 2, i]
                if r == ROWS - 1:
                    total += (high_edge * NU) * halo[stage, 3, i]
                step = weight * dt[pl.ds(dbase + r * 8, 8), :]
                target[pl.ds(base + r * 8, 8), :] = (
                    partial[pl.ds(base + r * 8, 8), :] + step * total)
            return carry
        lax.fori_loop(0, WV, body, 0)

    def speed_lanes(k, j):
        def of(w, v):
            return speeds[k, w, v] if v < NV else 0.0
        return jnp.where(sub < 4,
                         jnp.where(lane < 64, of(0, 2 * j), of(0, 2 * j + 1)),
                         jnp.where(lane < 64, of(1, 2 * j), of(1, 2 * j + 1)))

    def interface_coefs():
        coefs = []
        for j in range(3):
            nu = NU if j < 2 else jnp.where(lane < 64, NU, 0.0)
            a0, a1, a2 = (speed_lanes(k, j) for k in range(3))
            coefs.append((-(a0 + a1 + a2) - 6.0 * nu,
                          jnp.where(sub == 4, 0.0, a0 + nu), jnp.where(sub == 3, 0.0, nu),
                          a1 + nu, nu, a2 + nu, nu))
        return coefs

    cell = lax.rem(lane, 8)
    row = lax.rem(lane, 64) // 8

    def interface_section(source, weight, coefs, s):
        before = lax.rem(s + slabs - 1, slabs)
        after = lax.rem(s + 1, slabs)
        result = []
        for d in range(3):
            last = inter[d, s, 2]
            step = weight * jnp.where(lane < 64, pltpu.roll(last, 64, 1), last)
            parts = []
            for j in range(3):
                c, xl, xh, rl, rh, pl_, ph = coefs[j]
                q = source[d, s, j]
                total = c * q + xl * pltpu.roll(q, 1, 0) + xh * pltpu.roll(q, 7, 0)
                total += pl_ * jnp.where(cell == 0, pltpu.roll(source[d, before, j], 121, 1),
                                         pltpu.roll(q, 1, 1))
                total += ph * jnp.where(cell == 7, pltpu.roll(source[d, after, j], 7, 1),
                                        pltpu.roll(q, 127, 1))
                low = pltpu.roll(q, 8, 1)
                if d > 0:
                    low = jnp.where(row == 0, pltpu.roll(source[d - 1, s, j], 72, 1), low)
                high = pltpu.roll(q, 120, 1)
                if d < 2:
                    high = jnp.where(row == 7, pltpu.roll(source[d + 1, s, j], 56, 1), high)
                total += rl * low + rh * high
                parts.append(inter[d, s, j] + step * total)
            result.append(parts)
        return result

    def interface_step(source, target, weight):
        def body(s, carry):
            coefs = interface_coefs()
            result = interface_section(source, weight, coefs, s)
            for d in range(3):
                for j in range(3):
                    target[d, s, j] = result[d][j]
            return carry
        lax.fori_loop(0, slabs, body, 0)

    def interface_last(source, weight):
        near = (lax.broadcasted_iota(jnp.int32, (8, 8), 0)
                == lax.broadcasted_iota(jnp.int32, (8, 8), 1))

        def column(ref, slot, w):
            line = jnp.broadcast_to(ref[slot, w:w + 1, :].astype(jnp.float32), (8, 8))
            return jnp.sum(jnp.where(near, line, 0.0), axis=1, keepdims=True)
        columns_of = [[(column(src_ref, slot, w), column(frac_ref, slot, w) * (1.0 / 65536.0))
                       for slot in range(3)] for w in range(2)]
        shares = []
        for w in range(2):
            per_block = []
            for d in range(3):
                place = ((b + d - 1) * ROWS + row).astype(jnp.float32)
                share = jnp.zeros((8, 128), jnp.float32)
                for origin, fraction in columns_of[w]:
                    share += jnp.where(origin == place, fraction, 0.0)
                per_block.append(share)
            shares.append(per_block)

        def body(s, total):
            coefs = interface_coefs()
            result = interface_section(source, weight, coefs, s)
            sides = []
            for w in range(2):
                at = 4 if w == 0 else 3
                columns = []
                for j in range(3):
                    columns.append(sum(jnp.broadcast_to(result[d][j][at:at + 1, :], (8, 128))
                                       * shares[w][d] for d in range(3)))
                sides.append(jnp.concatenate(columns, 1))
            lhs = jnp.concatenate(sides, 0)
            waves = []
            for v in range(NV):
                waves += [table[s, v]] * ROWS
            waves.append(jnp.zeros((64, 128), jnp.float32))
            rhs = jnp.concatenate(waves, 0)
            return total + jnp.dot(lhs, rhs, precision=HIGHEST,
                                   preferred_element_type=jnp.float32)
        total = lax.fori_loop(0, slabs, body, jnp.zeros((16, 128), jnp.float32))
        columns = arr_ref.shape[2]
        arr_ref[0] = total[0:8, 0:columns]
        arr_ref[1] = total[8:16, 0:columns]

    w1, w2, w3 = section_weights
    loads[3].wait()
    inner(q0, w1)
    for copy in stages[0]:
        copy.wait_recv()
    outer(0, field, w1)
    pack(field, 1)
    for copy in stages[1]:
        copy.start()

    inner(field, w2)
    for copy in gathers:
        copy.wait_send()
    for copy in gathers:
        copy.wait_recv()

    def edges(s, carry):
        for j in range(3):
            inter[0, s, j] = inter[0, s, j] * low_edge
            inter[2, s, j] = inter[2, s, j] * high_edge
        return carry
    lax.fori_loop(0, slabs, edges, 0)
    interface_step(inter, inter_b, w1)
    for copy in stages[1]:
        copy.wait_recv()
    outer(1, field, w2)
    pack(field, 2)
    for copy in stages[2]:
        copy.start()

    inner(field, w3)
    interface_step(inter_b, inter_c, w2)
    for load in (loads[2], loads[4], loads[5]):
        load.wait()
    interface_last(inter_c, w3)
    for copy in stages[2]:
        copy.wait_recv()
    outer(2, out_ref, w3)
    for stage in stages:
        for copy in stage:
            copy.wait_send()


def shards(tables, states, time_steps, speeds, band_src, band_frac):
    blocks = lax.axis_size("blk")
    slabs = lax.axis_size("pitch")
    any_space = pl.BlockSpec(memory_space=pl.ANY)
    vmem = pl.BlockSpec(memory_space=pltpu.VMEM)
    cells = WV * ROWS * 8
    columns = NV * 2 * NH // slabs
    field, arrivals = pl.pallas_call(
        functools.partial(kernel, blocks, slabs),
        out_shape=(pltpu.VMEM((cells, 128), jnp.float32),
                   pltpu.VMEM((2, ROWS, columns), jnp.float32)),
        in_specs=[any_space] * 6,
        out_specs=(vmem, vmem),
        scratch_shapes=[
            pltpu.SMEM((3, 2, NV), jnp.float32),
            pltpu.VMEM((3, 2, ROWS), jnp.int32),
            pltpu.VMEM((3, 2, ROWS), jnp.int32),
            pltpu.VMEM((cells, 128), jnp.float32),
            pltpu.VMEM((128, 128), jnp.float32),
            pltpu.VMEM((slabs, NV, 8, 128), jnp.float32),
            pltpu.VMEM((cells, 128), jnp.float32),
            pltpu.VMEM((cells, 128), jnp.float32),
            pltpu.VMEM((3, 4, WV, 8, 128), jnp.float32),
            pltpu.VMEM((3, 4, WV, 8, 128), jnp.float32),
            pltpu.VMEM((3, slabs, 3, 8, 128), jnp.float32),
            pltpu.VMEM((3, slabs, 3, 8, 128), jnp.float32),
            pltpu.VMEM((3, slabs, 3, 8, 128), jnp.float32),
            pltpu.SemaphoreType.DMA((6,)),
            pltpu.SemaphoreType.DMA((3, 4)),
            pltpu.SemaphoreType.DMA((3, 4)),
            pltpu.SemaphoreType.DMA((len(PEERS),)),
            pltpu.SemaphoreType.DMA((len(PEERS),)),
        ],
        compiler_params=pltpu.CompilerParams(collective_id=0, has_side_effects=True),
        name="window",
    )(jnp.transpose(speeds, (2, 0, 1)), states.reshape(cells, 128), time_steps.reshape(128, 128),
      jnp.asarray(tables), jnp.transpose(band_src, (2, 0, 1)), jnp.transpose(band_frac, (2, 0, 1)))
    return field.reshape(states.shape), arrivals


def solution(mesh):
    tables = harmonic_tables(mesh.shape["pitch"], 8)
    return jax.shard_map(
        functools.partial(shards, tables),
        mesh=mesh,
        in_specs=(
            P(None, None, "blk", "pitch", None),
            P(None, "blk", "pitch", None),
            P(),
            P(None, "blk", None),
            P(None, "blk", None),
        ),
        out_specs=(P(None, None, "blk", "pitch", None), P(None, "blk", "pitch")),
        check_vma=False,
    )
```

```python
import functools

import jax
import jax.numpy as jnp
import numpy as np
from jax import lax
from jax.experimental import pallas as pl
from jax.experimental.pallas import tpu as pltpu
from jax.sharding import PartitionSpec as P

NH = 48
NV = 5
WV = 2 * NV
ROWS = 8
NU = 0.15
section_weights = (1.0 / 3.0, 0.5, 1.0)
MESH = pl.DeviceIdType.MESH
HIGHEST = lax.Precision.HIGHEST
PEERS = [(db, dx) for db in (0, -1, 1) for dx in (0, 1, 3, 2) if (db, dx) != (0, 0)]


def harmonic_tables(slabs, slab):
    period = slabs * slab
    places = np.arange(period)[:, None]
    orders = np.arange(NH)[None, :]
    factor = np.where(orders == 0, 1.0, 2.0) / period
    cos_cols = np.cos(2.0 * np.pi * (places * orders % period) / period) * factor
    sin_cols = np.sin(2.0 * np.pi * (places * (orders + 1) % period) / period) * (2.0 / period)
    table = np.concatenate([cos_cols, sin_cols], 1)
    total = NV * 2 * NH
    chunk = total // slabs
    full = np.zeros((NV, period, total))
    for v in range(NV):
        full[v, :, v * 2 * NH:(v + 1) * 2 * NH] = table
    full = full.reshape(NV, slabs, slab, slabs, chunk).transpose(3, 1, 0, 2, 4)
    out = np.zeros((slabs, slabs, NV, slab, 128), np.float32)
    out[..., :chunk] = full
    return out


def kernel(blocks, slabs, speeds_hbm, states_hbm, steps_hbm, table_hbm, src_hbm, frac_hbm,
           out_ref, arr_ref,
           speeds, src_ref, frac_ref, q0, dt, table, partial, field, send, halo, inter, inter_b, inter_c,
           load_sem, send_sem, recv_sem, isend_sem, irecv_sem):
    b = lax.axis_index("blk")
    x = lax.axis_index("pitch")

    def device(db, dx):
        return {"blk": lax.rem(b + db + blocks, blocks), "pitch": lax.rem(x + dx + slabs, slabs)}

    barrier = pltpu.get_barrier_semaphore()

    def where_blocks(db, action):
        if db == 0:
            action()
        else:
            pl.when(b > 0 if db < 0 else b < blocks - 1)(action)

    def greet(db):
        for peer in PEERS:
            if peer[0] == db:
                pl.semaphore_signal(barrier, inc=1, device_id=device(*peer), device_id_type=MESH)
    for db in (0, -1, 1):
        where_blocks(db, functools.partial(greet, db))
    loads = [
        pltpu.make_async_copy(states_hbm, q0, load_sem.at[0]),
        pltpu.make_async_copy(steps_hbm, dt, load_sem.at[1]),
        pltpu.make_async_copy(table_hbm.at[x], table, load_sem.at[2]),
        pltpu.make_async_copy(speeds_hbm, speeds, load_sem.at[3]),
        pltpu.make_async_copy(src_hbm, src_ref, load_sem.at[4]),
        pltpu.make_async_copy(frac_hbm, frac_ref, load_sem.at[5]),
    ]
    for load in loads:
        load.start()

    lane = lax.broadcasted_iota(jnp.int32, (8, 128), 1)
    sub = lax.broadcasted_iota(jnp.int32, (8, 128), 0)

    @pl.when(b == 0)
    def _():
        for stage in range(3):
            halo[stage, 2] = jnp.zeros((WV, 8, 128), jnp.float32)
        inter[0] = jnp.zeros(inter.shape[1:], jnp.float32)

    @pl.when(b == blocks - 1)
    def _():
        for stage in range(3):
            halo[stage, 3] = jnp.zeros((WV, 8, 128), jnp.float32)
        inter[2] = jnp.zeros(inter.shape[1:], jnp.float32)

    def pack(source, stage, i):
        base = pl.multiple_of(i * 64, 64)
        send[stage, 0, i] = source[pl.ds(base + 7, 8, stride=8), :]
        send[stage, 1, i] = source[pl.ds(base, 8, stride=8), :]
        send[stage, 2, i] = source[pl.ds(base + 56, 8), :]
        send[stage, 3, i] = source[pl.ds(base, 8), :]

    def exchange(stage):
        copies = []
        for d, (db, dx) in enumerate(((0, 1), (0, -1), (1, 0), (-1, 0))):
            copies.append((db, pltpu.make_async_remote_copy(
                src_ref=send.at[stage, d], dst_ref=halo.at[stage, d],
                send_sem=send_sem.at[stage, d], recv_sem=recv_sem.at[stage, d],
                device_id=device(db, dx), device_id_type=MESH)))
        return copies

    def start(copies):
        for sign in (1, -1, 0):
            chosen = [copy for db, copy in copies if db == sign]
            where_blocks(sign, lambda: [copy.start() for copy in chosen] and None)

    def wait_recv(copies):
        for sign in (0, 1, -1):
            chosen = [copy for db, copy in copies if db == sign]
            where_blocks(-sign, lambda: [copy.wait_recv() for copy in chosen] and None)

    def wait_send(copies):
        for sign in (0, 1, -1):
            chosen = [copy for db, copy in copies if db == sign]
            where_blocks(sign, lambda: [copy.wait_send() for copy in chosen] and None)

    loads[0].wait()
    loads[1].wait()

    def pack_body(i, carry):
        pack(q0, 0, i)
        return carry
    lax.fori_loop(0, WV, pack_body, 0)
    below = (b + blocks - 1) // blocks
    above = (2 * blocks - 2 - b) // blocks
    pl.semaphore_wait(barrier, slabs - 1 + slabs * (below + above))
    stages = [exchange(stage) for stage in range(3)]
    start(stages[0])
    chosen = []
    for w in range(2):
        first = 124 if w == 0 else -4
        pick = jnp.where((sub // 4 == w) & (lane == sub + first), 1.0, 0.0)
        cells = jnp.concatenate([q0[w * 320:(w + 1) * 320, :], dt[w * 64:(w + 1) * 64, :]], 0)
        chosen.append(lax.dot_general(pick, cells, (((1,), (1,)), ((), ())),
                                      precision=HIGHEST, preferred_element_type=jnp.float32))
    packet = chosen[0] + chosen[1]
    for j in range(3):
        inter[1, x, j] = packet[:, j * 128:(j + 1) * 128]

    gathers = []
    for k, (db, dx) in enumerate(PEERS):
        gathers.append((db, pltpu.make_async_remote_copy(
            src_ref=inter.at[1, x], dst_ref=inter.at[1 - db, x],
            send_sem=isend_sem.at[k], recv_sem=irecv_sem.at[k],
            device_id=device(db, dx), device_id_type=MESH)))
    start(gathers)

    def inner(source, weight):
        def body(i, carry):
            base = pl.multiple_of(i * 64, 64)
            dbase = pl.multiple_of((i // NV) * 64, 64)
            a0, a1, a2 = (speeds[k, i // NV, lax.rem(i, NV)] for k in range(3))
            centre = -(a0 + a1 + a2) - 6.0 * NU
            axial_low = jnp.where(lane == 0, 0.0, a0 + NU)
            axial_high = jnp.where(lane == 127, 0.0, NU)
            pitch_low = jnp.where(sub == 0, 0.0, a2 + NU)
            pitch_high = jnp.where(sub == 7, 0.0, NU)
            rows = [source[pl.ds(base + r * 8, 8), :] for r in range(ROWS)]
            for r in range(ROWS):
                q = rows[r]
                total = centre * q
                total += axial_low * pltpu.roll(q, 1, 1)
                total += axial_high * pltpu.roll(q, 127, 1)
                total += pitch_low * pltpu.roll(q, 1, 0)
                total += pitch_high * pltpu.roll(q, 7, 0)
                if r > 0:
                    total += (a1 + NU) * rows[r - 1]
                if r < ROWS - 1:
                    total += NU * rows[r + 1]
                step = weight * dt[pl.ds(dbase + r * 8, 8), :]
                partial[pl.ds(base + r * 8, 8), :] = q0[pl.ds(base + r * 8, 8), :] + step * total
            return carry
        lax.fori_loop(0, WV, body, 0)

    def outer(stage, target, weight):
        def body(i, carry):
            base = pl.multiple_of(i * 64, 64)
            dbase = pl.multiple_of((i // NV) * 64, 64)
            a1, a2 = (speeds[k, i // NV, lax.rem(i, NV)] for k in range(1, 3))
            pitch_low = jnp.where(sub == 0, a2 + NU, 0.0)
            pitch_high = jnp.where(sub == 7, NU, 0.0)
            for r in range(ROWS):
                total = pitch_low * halo[stage, 0, i, pl.ds(r, 1), :]
                total += pitch_high * halo[stage, 1, i, pl.ds(r, 1), :]
                if r == 0:
                    total += (a1 + NU) * halo[stage, 2, i]
                if r == ROWS - 1:
                    total += NU * halo[stage, 3, i]
                step = weight * dt[pl.ds(dbase + r * 8, 8), :]
                target[pl.ds(base + r * 8, 8), :] = (
                    partial[pl.ds(base + r * 8, 8), :] + step * total)
            if stage < 2:
                pack(target, stage + 1, i)
            return carry
        lax.fori_loop(0, WV, body, 0)

    def speed_lanes(k, j):
        def of(w, v):
            return speeds[k, w, v] if v < NV else 0.0
        return jnp.where(sub < 4,
                         jnp.where(lane < 64, of(0, 2 * j), of(0, 2 * j + 1)),
                         jnp.where(lane < 64, of(1, 2 * j), of(1, 2 * j + 1)))

    def interface_coefs():
        coefs = []
        for j in range(3):
            nu = NU if j < 2 else jnp.where(lane < 64, NU, 0.0)
            a0, a1, a2 = (speed_lanes(k, j) for k in range(3))
            coefs.append((-(a0 + a1 + a2) - 6.0 * nu,
                          jnp.where(sub == 4, 0.0, a0 + nu), jnp.where(sub == 3, 0.0, nu),
                          a1 + nu, nu, a2 + nu, nu))
        return coefs

    cell = lax.rem(lane, 8)
    row = lax.rem(lane, 64) // 8

    def interface_section(source, weight, coefs, s):
        before = lax.rem(s + slabs - 1, slabs)
        after = lax.rem(s + 1, slabs)
        result = []
        for d in range(3):
            last = inter[d, s, 2]
            step = weight * jnp.where(lane < 64, pltpu.roll(last, 64, 1), last)
            parts = []
            for j in range(3):
                c, xl, xh, rl, rh, pl_, ph = coefs[j]
                q = source[d, s, j]
                total = c * q + xl * pltpu.roll(q, 1, 0) + xh * pltpu.roll(q, 7, 0)
                total += pl_ * jnp.where(cell == 0, pltpu.roll(source[d, before, j], 121, 1),
                                         pltpu.roll(q, 1, 1))
                total += ph * jnp.where(cell == 7, pltpu.roll(source[d, after, j], 7, 1),
                                        pltpu.roll(q, 127, 1))
                low = pltpu.roll(q, 8, 1)
                if d > 0:
                    low = jnp.where(row == 0, pltpu.roll(source[d - 1, s, j], 72, 1), low)
                high = pltpu.roll(q, 120, 1)
                if d < 2:
                    high = jnp.where(row == 7, pltpu.roll(source[d + 1, s, j], 56, 1), high)
                total += rl * low + rh * high
                parts.append(inter[d, s, j] + step * total)
            result.append(parts)
        return result

    def interface_step(source, target, weight):
        def body(s, carry):
            coefs = interface_coefs()
            result = interface_section(source, weight, coefs, s)
            for d in range(3):
                for j in range(3):
                    target[d, s, j] = result[d][j]
            return carry
        lax.fori_loop(0, slabs, body, 0)

    def interface_last(source, weight):
        near = (lax.broadcasted_iota(jnp.int32, (8, 8), 0)
                == lax.broadcasted_iota(jnp.int32, (8, 8), 1))

        def column(ref, slot, w):
            line = jnp.broadcast_to(ref[slot, w:w + 1, :].astype(jnp.float32), (8, 8))
            return jnp.sum(jnp.where(near, line, 0.0), axis=1, keepdims=True)
        columns_of = [[(column(src_ref, slot, w), column(frac_ref, slot, w) * (1.0 / 65536.0))
                       for slot in range(3)] for w in range(2)]
        shares = []
        for w in range(2):
            per_block = []
            for d in range(3):
                place = ((b + d - 1) * ROWS + row).astype(jnp.float32)
                share = jnp.zeros((8, 128), jnp.float32)
                for origin, fraction in columns_of[w]:
                    share += jnp.where(origin == place, fraction, 0.0)
                per_block.append(share)
            shares.append(per_block)

        def body(s, total):
            coefs = interface_coefs()
            result = interface_section(source, weight, coefs, s)
            sides = []
            for w in range(2):
                at = 4 if w == 0 else 3
                columns = []
                for j in range(3):
                    columns.append(sum(jnp.broadcast_to(result[d][j][at:at + 1, :], (8, 128))
                                       * shares[w][d] for d in range(3)))
                sides.append(jnp.concatenate(columns, 1))
            lhs = jnp.concatenate(sides, 0)
            waves = []
            for v in range(NV):
                waves += [table[s, v]] * ROWS
            waves.append(jnp.zeros((64, 128), jnp.float32))
            rhs = jnp.concatenate(waves, 0)
            return total + jnp.dot(lhs, rhs, precision=HIGHEST,
                                   preferred_element_type=jnp.float32)
        total = lax.fori_loop(0, slabs, body, jnp.zeros((16, 128), jnp.float32))
        columns = arr_ref.shape[2]
        arr_ref[0] = total[0:8, 0:columns]
        arr_ref[1] = total[8:16, 0:columns]

    w1, w2, w3 = section_weights
    loads[3].wait()
    inner(q0, w1)
    wait_recv(stages[0])
    outer(0, field, w1)
    start(stages[1])

    inner(field, w2)
    wait_recv(gathers)
    interface_step(inter, inter_b, w1)
    wait_recv(stages[1])
    outer(1, field, w2)
    start(stages[2])

    inner(field, w3)
    interface_step(inter_b, inter_c, w2)
    for load in (loads[2], loads[4], loads[5]):
        load.wait()
    interface_last(inter_c, w3)
    wait_send(gathers)
    for stage in stages[:2]:
        wait_send(stage)
    wait_recv(stages[2])
    outer(2, out_ref, w3)
    wait_send(stages[2])


def write_out(field_ref, arr_ref, field_hbm, arr_hbm, sems):
    quarter = field_ref.shape[0] // 4
    copies = [pltpu.make_async_copy(field_ref.at[pl.ds(k * quarter, quarter)],
                                    field_hbm.at[pl.ds(k * quarter, quarter)], sems.at[k])
              for k in range(4)]
    copies.append(pltpu.make_async_copy(arr_ref, arr_hbm, sems.at[4]))
    for copy in copies:
        copy.start()
    for copy in copies:
        copy.wait()


def shards(tables, states, time_steps, speeds, band_src, band_frac):
    blocks = lax.axis_size("blk")
    slabs = lax.axis_size("pitch")
    any_space = pl.BlockSpec(memory_space=pl.ANY)
    vmem = pl.BlockSpec(memory_space=pltpu.VMEM)
    cells = WV * ROWS * 8
    columns = NV * 2 * NH // slabs
    field, arrivals = pl.pallas_call(
        functools.partial(kernel, blocks, slabs),
        out_shape=(pltpu.VMEM((cells, 128), jnp.float32),
                   pltpu.VMEM((2, ROWS, columns), jnp.float32)),
        in_specs=[any_space] * 6,
        out_specs=(vmem, vmem),
        scratch_shapes=[
            pltpu.SMEM((3, 2, NV), jnp.float32),
            pltpu.VMEM((3, 2, ROWS), jnp.int32),
            pltpu.VMEM((3, 2, ROWS), jnp.int32),
            pltpu.VMEM((cells, 128), jnp.float32),
            pltpu.VMEM((128, 128), jnp.float32),
            pltpu.VMEM((slabs, NV, 8, 128), jnp.float32),
            pltpu.VMEM((cells, 128), jnp.float32),
            pltpu.VMEM((cells, 128), jnp.float32),
            pltpu.VMEM((3, 4, WV, 8, 128), jnp.float32),
            pltpu.VMEM((3, 4, WV, 8, 128), jnp.float32),
            pltpu.VMEM((3, slabs, 3, 8, 128), jnp.float32),
            pltpu.VMEM((3, slabs, 3, 8, 128), jnp.float32),
            pltpu.VMEM((3, slabs, 3, 8, 128), jnp.float32),
            pltpu.SemaphoreType.DMA((6,)),
            pltpu.SemaphoreType.DMA((3, 4)),
            pltpu.SemaphoreType.DMA((3, 4)),
            pltpu.SemaphoreType.DMA((len(PEERS),)),
            pltpu.SemaphoreType.DMA((len(PEERS),)),
        ],
        compiler_params=pltpu.CompilerParams(collective_id=0, has_side_effects=True),
        name="window",
    )(jnp.transpose(speeds, (2, 0, 1)), states.reshape(cells, 128), time_steps.reshape(128, 128),
      jnp.asarray(tables), jnp.transpose(band_src, (2, 0, 1)), jnp.transpose(band_frac, (2, 0, 1)))
    field, arrivals = pl.pallas_call(
        write_out,
        out_shape=(jax.ShapeDtypeStruct(field.shape, jnp.float32),
                   jax.ShapeDtypeStruct(arrivals.shape, jnp.float32)),
        in_specs=[vmem] * 2,
        out_specs=(any_space, any_space),
        scratch_shapes=[pltpu.SemaphoreType.DMA((5,))],
        name="write_out",
    )(pltpu.with_memory_space_constraint(field, pltpu.VMEM),
      pltpu.with_memory_space_constraint(arrivals, pltpu.VMEM))
    return field.reshape(states.shape), arrivals


def solution(mesh):
    tables = harmonic_tables(mesh.shape["pitch"], 8)
    return jax.shard_map(
        functools.partial(shards, tables),
        mesh=mesh,
        in_specs=(
            P(None, None, "blk", "pitch", None),
            P(None, "blk", "pitch", None),
            P(),
            P(None, "blk", None),
            P(None, "blk", None),
        ),
        out_specs=(P(None, None, "blk", "pitch", None), P(None, "blk", "pitch")),
        check_vma=False,
    )
```

```python
import functools

import jax
import jax.numpy as jnp
import numpy as np
from jax import lax
from jax.experimental import pallas as pl
from jax.experimental.pallas import tpu as pltpu
from jax.sharding import PartitionSpec as P

NH = 48
NV = 5
WV = 2 * NV
ROWS = 8
NU = 0.15
section_weights = (1.0 / 3.0, 0.5, 1.0)
MESH = pl.DeviceIdType.MESH
HIGHEST = lax.Precision.HIGHEST
NEAR = ((0, 1), (0, -1), (1, 0), (-1, 0))
RELAYS = (((0, 1, 0), (0, -1, 0), (0, 0, 1), (0, 0, -1)),
          ((-1, 0, 1), (-1, 1, 0), (-1, -1, 0), (1, 1, 0), (1, -1, 0)),
          ((2, 1, 0), (2, -1, 0)))


def harmonic_tables(slabs, slab):
    period = slabs * slab
    places = np.arange(period)[:, None]
    orders = np.arange(NH)[None, :]
    factor = np.where(orders == 0, 1.0, 2.0) / period
    cos_cols = np.cos(2.0 * np.pi * (places * orders % period) / period) * factor
    sin_cols = np.sin(2.0 * np.pi * (places * (orders + 1) % period) / period) * (2.0 / period)
    table = np.concatenate([cos_cols, sin_cols], 1)
    total = NV * 2 * NH
    chunk = total // slabs
    full = np.zeros((NV, period, total))
    for v in range(NV):
        full[v, :, v * 2 * NH:(v + 1) * 2 * NH] = table
    full = full.reshape(NV, slabs, slab, slabs, chunk).transpose(3, 1, 0, 2, 4)
    out = np.zeros((slabs, slabs, NV, slab, 128), np.float32)
    out[..., :chunk] = full
    return out


def kernel(blocks, slabs, speeds_hbm, blocks_hbm, states_hbm, steps_hbm, table_hbm, src_hbm, frac_hbm,
           out_ref, arr_ref,
           speeds, src_ref, frac_ref, q0, dt, table, partial, field, send, halo, inter, inter_b, inter_c,
           load_sem, send_sem, recv_sem, isend_sem, irecv_sem):
    b = lax.axis_index("blk")
    x = lax.axis_index("pitch")

    def device(db, dx):
        return {"blk": lax.rem(b + db + blocks, blocks), "pitch": lax.rem(x + dx + slabs, slabs)}

    barrier = pltpu.get_barrier_semaphore()

    def where_blocks(db, action):
        if db == 0:
            action()
        else:
            pl.when(b > 0 if db < 0 else b < blocks - 1)(action)

    def greet(db):
        for peer in NEAR:
            if peer[0] == db:
                pl.semaphore_signal(barrier, inc=1, device_id=device(*peer), device_id_type=MESH)
    for db in (0, -1, 1):
        where_blocks(db, functools.partial(greet, db))
    loads = [
        pltpu.make_async_copy(states_hbm, q0, load_sem.at[0]),
        pltpu.make_async_copy(steps_hbm, dt, load_sem.at[1]),
        pltpu.make_async_copy(table_hbm.at[x], table, load_sem.at[2]),
        pltpu.make_async_copy(speeds_hbm, speeds, load_sem.at[3]),
        pltpu.make_async_copy(src_hbm, src_ref, load_sem.at[4]),
        pltpu.make_async_copy(frac_hbm, frac_ref, load_sem.at[5]),
    ]
    for load in loads:
        load.start()

    lane = lax.broadcasted_iota(jnp.int32, (8, 128), 1)
    sub = lax.broadcasted_iota(jnp.int32, (8, 128), 0)

    @pl.when(b == 0)
    def _():
        for stage in range(3):
            halo[stage, 2] = jnp.zeros((WV, 8, 128), jnp.float32)
        inter[0] = jnp.zeros(inter.shape[1:], jnp.float32)

    @pl.when(b == blocks - 1)
    def _():
        for stage in range(3):
            halo[stage, 3] = jnp.zeros((WV, 8, 128), jnp.float32)
        inter[2] = jnp.zeros(inter.shape[1:], jnp.float32)

    def pack(source, stage, i):
        base = pl.multiple_of(i * 64, 64)
        send[stage, 0, i] = source[pl.ds(base + 7, 8, stride=8), :]
        send[stage, 1, i] = source[pl.ds(base, 8, stride=8), :]
        send[stage, 2, i] = source[pl.ds(base + 56, 8), :]
        send[stage, 3, i] = source[pl.ds(base, 8), :]

    faces = (blocks_hbm.at[:, :, 7], blocks_hbm.at[:, :, 0],
             blocks_hbm.at[:, ROWS - 1], blocks_hbm.at[:, 0])

    def exchange(stage):
        copies = []
        for d, (db, dx) in enumerate(NEAR):
            copies.append((db, pltpu.make_async_remote_copy(
                src_ref=faces[d] if stage == 0 else send.at[stage - 1, d], dst_ref=halo.at[stage, d],
                send_sem=send_sem.at[stage, d], recv_sem=recv_sem.at[stage, d],
                device_id=device(db, dx), device_id_type=MESH)))
        return copies

    def start(copies):
        for sign in (1, -1, 0):
            chosen = [copy for db, copy in copies if db == sign]
            where_blocks(sign, lambda: [copy.start() for copy in chosen] and None)

    def wait_recv(copies):
        for sign in (0, 1, -1):
            chosen = [copy for db, copy in copies if db == sign]
            where_blocks(-sign, lambda: [copy.wait_recv() for copy in chosen] and None)

    def wait_send(copies):
        for sign in (0, 1, -1):
            chosen = [copy for db, copy in copies if db == sign]
            where_blocks(sign, lambda: [copy.wait_send() for copy in chosen] and None)

    below = (b + blocks - 1) // blocks
    above = (2 * blocks - 2 - b) // blocks
    pl.semaphore_wait(barrier, 2 + below + above)
    stages = [exchange(stage) for stage in range(3)]
    start(stages[0])
    loads[0].wait()
    loads[1].wait()
    chosen = []
    for w in range(2):
        first = 124 if w == 0 else -4
        pick = jnp.where((sub // 4 == w) & (lane == sub + first), 1.0, 0.0)
        cells = jnp.concatenate([q0[w * 320:(w + 1) * 320, :], dt[w * 64:(w + 1) * 64, :]], 0)
        chosen.append(lax.dot_general(pick, cells, (((1,), (1,)), ((), ())),
                                      precision=HIGHEST, preferred_element_type=jnp.float32))
    packet = chosen[0] + chosen[1]
    for j in range(3):
        inter[1, x, j] = packet[:, j * 128:(j + 1) * 128]

    gathers = []
    for phase in RELAYS:
        copies = []
        for slab, db, dx in phase:
            k = sum(len(done) for done in gathers) + len(copies)
            at = lax.rem(x + slab + slabs, slabs)
            copies.append((db, pltpu.make_async_remote_copy(
                src_ref=inter.at[1, at], dst_ref=inter.at[1 - db, at],
                send_sem=isend_sem.at[k], recv_sem=irecv_sem.at[k],
                device_id=device(db, dx), device_id_type=MESH)))
        gathers.append(copies)
    start(gathers[0])

    def inner(source, weight):
        def body(i, carry):
            base = pl.multiple_of(i * 64, 64)
            dbase = pl.multiple_of((i // NV) * 64, 64)
            a0, a1, a2 = (speeds[k, i // NV, lax.rem(i, NV)] for k in range(3))
            centre = -(a0 + a1 + a2) - 6.0 * NU
            axial_low = jnp.where(lane == 0, 0.0, a0 + NU)
            axial_high = jnp.where(lane == 127, 0.0, NU)
            pitch_low = jnp.where(sub == 0, 0.0, a2 + NU)
            pitch_high = jnp.where(sub == 7, 0.0, NU)
            rows = [source[pl.ds(base + r * 8, 8), :] for r in range(ROWS)]
            for r in range(ROWS):
                q = rows[r]
                total = centre * q
                total += axial_low * pltpu.roll(q, 1, 1)
                total += axial_high * pltpu.roll(q, 127, 1)
                total += pitch_low * pltpu.roll(q, 1, 0)
                total += pitch_high * pltpu.roll(q, 7, 0)
                if r > 0:
                    total += (a1 + NU) * rows[r - 1]
                if r < ROWS - 1:
                    total += NU * rows[r + 1]
                step = weight * dt[pl.ds(dbase + r * 8, 8), :]
                partial[pl.ds(base + r * 8, 8), :] = q0[pl.ds(base + r * 8, 8), :] + step * total
            return carry
        lax.fori_loop(0, WV, body, 0)

    def outer(stage, target, weight):
        def body(i, carry):
            base = pl.multiple_of(i * 64, 64)
            dbase = pl.multiple_of((i // NV) * 64, 64)
            a1, a2 = (speeds[k, i // NV, lax.rem(i, NV)] for k in range(1, 3))
            pitch_low = jnp.where(sub == 0, a2 + NU, 0.0)
            pitch_high = jnp.where(sub == 7, NU, 0.0)
            for r in range(ROWS):
                total = pitch_low * halo[stage, 0, i, pl.ds(r, 1), :]
                total += pitch_high * halo[stage, 1, i, pl.ds(r, 1), :]
                if r == 0:
                    total += (a1 + NU) * halo[stage, 2, i]
                if r == ROWS - 1:
                    total += NU * halo[stage, 3, i]
                step = weight * dt[pl.ds(dbase + r * 8, 8), :]
                target[pl.ds(base + r * 8, 8), :] = (
                    partial[pl.ds(base + r * 8, 8), :] + step * total)
            if stage < 2:
                pack(target, stage, i)
            return carry
        lax.fori_loop(0, WV, body, 0)

    def speed_lanes(k, j):
        def of(w, v):
            return speeds[k, w, v] if v < NV else 0.0
        return jnp.where(sub < 4,
                         jnp.where(lane < 64, of(0, 2 * j), of(0, 2 * j + 1)),
                         jnp.where(lane < 64, of(1, 2 * j), of(1, 2 * j + 1)))

    def interface_coefs():
        coefs = []
        for j in range(3):
            nu = NU if j < 2 else jnp.where(lane < 64, NU, 0.0)
            a0, a1, a2 = (speed_lanes(k, j) for k in range(3))
            coefs.append((-(a0 + a1 + a2) - 6.0 * nu,
                          jnp.where(sub == 4, 0.0, a0 + nu), jnp.where(sub == 3, 0.0, nu),
                          a1 + nu, nu, a2 + nu, nu))
        return coefs

    cell = lax.rem(lane, 8)
    row = lax.rem(lane, 64) // 8

    def interface_section(source, weight, coefs, s):
        before = lax.rem(s + slabs - 1, slabs)
        after = lax.rem(s + 1, slabs)
        result = []
        for d in range(3):
            last = inter[d, s, 2]
            step = weight * jnp.where(lane < 64, pltpu.roll(last, 64, 1), last)
            parts = []
            for j in range(3):
                c, xl, xh, rl, rh, pl_, ph = coefs[j]
                q = source[d, s, j]
                total = c * q + xl * pltpu.roll(q, 1, 0) + xh * pltpu.roll(q, 7, 0)
                total += pl_ * jnp.where(cell == 0, pltpu.roll(source[d, before, j], 121, 1),
                                         pltpu.roll(q, 1, 1))
                total += ph * jnp.where(cell == 7, pltpu.roll(source[d, after, j], 7, 1),
                                        pltpu.roll(q, 127, 1))
                low = pltpu.roll(q, 8, 1)
                if d > 0:
                    low = jnp.where(row == 0, pltpu.roll(source[d - 1, s, j], 72, 1), low)
                high = pltpu.roll(q, 120, 1)
                if d < 2:
                    high = jnp.where(row == 7, pltpu.roll(source[d + 1, s, j], 56, 1), high)
                total += rl * low + rh * high
                parts.append(inter[d, s, j] + step * total)
            result.append(parts)
        return result

    def interface_step(source, target, weight):
        def body(s, carry):
            coefs = interface_coefs()
            result = interface_section(source, weight, coefs, s)
            for d in range(3):
                for j in range(3):
                    target[d, s, j] = result[d][j]
            return carry
        lax.fori_loop(0, slabs, body, 0)

    def interface_last(source, weight):
        near = (lax.broadcasted_iota(jnp.int32, (8, 8), 0)
                == lax.broadcasted_iota(jnp.int32, (8, 8), 1))

        def column(ref, slot, w):
            line = jnp.broadcast_to(ref[slot, w:w + 1, :].astype(jnp.float32), (8, 8))
            return jnp.sum(jnp.where(near, line, 0.0), axis=1, keepdims=True)
        columns_of = [[(column(src_ref, slot, w), column(frac_ref, slot, w) * (1.0 / 65536.0))
                       for slot in range(3)] for w in range(2)]
        shares = []
        for w in range(2):
            per_block = []
            for d in range(3):
                place = ((b + d - 1) * ROWS + row).astype(jnp.float32)
                share = jnp.zeros((8, 128), jnp.float32)
                for origin, fraction in columns_of[w]:
                    share += jnp.where(origin == place, fraction, 0.0)
                per_block.append(share)
            shares.append(per_block)

        def body(s, total):
            coefs = interface_coefs()
            result = interface_section(source, weight, coefs, s)
            sides = []
            for w in range(2):
                at = 4 if w == 0 else 3
                columns = []
                for j in range(3):
                    columns.append(sum(jnp.broadcast_to(result[d][j][at:at + 1, :], (8, 128))
                                       * shares[w][d] for d in range(3)))
                sides.append(jnp.concatenate(columns, 1))
            lhs = jnp.concatenate(sides, 0)
            waves = []
            for v in range(NV):
                waves += [table[s, v]] * ROWS
            waves.append(jnp.zeros((64, 128), jnp.float32))
            rhs = jnp.concatenate(waves, 0)
            return total + jnp.dot(lhs, rhs, precision=HIGHEST,
                                   preferred_element_type=jnp.float32)
        total = lax.fori_loop(0, slabs, body, jnp.zeros((16, 128), jnp.float32))
        columns = arr_ref.shape[2]
        arr_ref[0] = total[0:8, 0:columns]
        arr_ref[1] = total[8:16, 0:columns]

    w1, w2, w3 = section_weights
    loads[3].wait()
    inner(q0, w1)
    wait_recv(gathers[0])
    start(gathers[1])
    wait_recv(stages[0])
    outer(0, field, w1)
    start(stages[1])

    inner(field, w2)
    wait_recv(gathers[1])
    start(gathers[2])
    wait_recv(stages[1])
    outer(1, field, w2)
    start(stages[2])

    inner(field, w3)
    wait_recv(gathers[2])
    interface_step(inter, inter_b, w1)
    interface_step(inter_b, inter_c, w2)
    for load in (loads[2], loads[4], loads[5]):
        load.wait()
    interface_last(inter_c, w3)
    for copies in gathers + stages[:2]:
        wait_send(copies)
    wait_recv(stages[2])
    outer(2, out_ref, w3)
    wait_send(stages[2])


def write_out(field_ref, arr_ref, field_hbm, arr_hbm, sems):
    quarter = field_ref.shape[0] // 4
    copies = [pltpu.make_async_copy(field_ref.at[pl.ds(k * quarter, quarter)],
                                    field_hbm.at[pl.ds(k * quarter, quarter)], sems.at[k])
              for k in range(4)]
    copies.append(pltpu.make_async_copy(arr_ref, arr_hbm, sems.at[4]))
    for copy in copies:
        copy.start()
    for copy in copies:
        copy.wait()


def shards(tables, states, time_steps, speeds, band_src, band_frac):
    blocks = lax.axis_size("blk")
    slabs = lax.axis_size("pitch")
    any_space = pl.BlockSpec(memory_space=pl.ANY)
    vmem = pl.BlockSpec(memory_space=pltpu.VMEM)
    cells = WV * ROWS * 8
    columns = NV * 2 * NH // slabs
    field, arrivals = pl.pallas_call(
        functools.partial(kernel, blocks, slabs),
        out_shape=(pltpu.VMEM((cells, 128), jnp.float32),
                   pltpu.VMEM((2, ROWS, columns), jnp.float32)),
        in_specs=[any_space] * 7,
        out_specs=(vmem, vmem),
        scratch_shapes=[
            pltpu.SMEM((3, 2, NV), jnp.float32),
            pltpu.VMEM((3, 2, ROWS), jnp.int32),
            pltpu.VMEM((3, 2, ROWS), jnp.int32),
            pltpu.VMEM((cells, 128), jnp.float32),
            pltpu.VMEM((128, 128), jnp.float32),
            pltpu.VMEM((slabs, NV, 8, 128), jnp.float32),
            pltpu.VMEM((cells, 128), jnp.float32),
            pltpu.VMEM((cells, 128), jnp.float32),
            pltpu.VMEM((2, 4, WV, 8, 128), jnp.float32),
            pltpu.VMEM((3, 4, WV, 8, 128), jnp.float32),
            pltpu.VMEM((3, slabs, 3, 8, 128), jnp.float32),
            pltpu.VMEM((3, slabs, 3, 8, 128), jnp.float32),
            pltpu.VMEM((3, slabs, 3, 8, 128), jnp.float32),
            pltpu.SemaphoreType.DMA((6,)),
            pltpu.SemaphoreType.DMA((3, 4)),
            pltpu.SemaphoreType.DMA((3, 4)),
            pltpu.SemaphoreType.DMA((sum(len(phase) for phase in RELAYS),)),
            pltpu.SemaphoreType.DMA((sum(len(phase) for phase in RELAYS),)),
        ],
        compiler_params=pltpu.CompilerParams(collective_id=0, has_side_effects=True),
        name="window",
    )(jnp.transpose(speeds, (2, 0, 1)), states.reshape(WV, ROWS, 8, 128),
      states.reshape(cells, 128), time_steps.reshape(128, 128),
      jnp.asarray(tables), jnp.transpose(band_src, (2, 0, 1)), jnp.transpose(band_frac, (2, 0, 1)))
    field, arrivals = pl.pallas_call(
        write_out,
        out_shape=(jax.ShapeDtypeStruct(field.shape, jnp.float32),
                   jax.ShapeDtypeStruct(arrivals.shape, jnp.float32)),
        in_specs=[vmem] * 2,
        out_specs=(any_space, any_space),
        scratch_shapes=[pltpu.SemaphoreType.DMA((5,))],
        name="write_out",
    )(pltpu.with_memory_space_constraint(field, pltpu.VMEM),
      pltpu.with_memory_space_constraint(arrivals, pltpu.VMEM))
    return field.reshape(states.shape), arrivals


def solution(mesh):
    tables = harmonic_tables(mesh.shape["pitch"], 8)
    return jax.shard_map(
        functools.partial(shards, tables),
        mesh=mesh,
        in_specs=(
            P(None, None, "blk", "pitch", None),
            P(None, "blk", "pitch", None),
            P(),
            P(None, "blk", None),
            P(None, "blk", None),
        ),
        out_specs=(P(None, None, "blk", "pitch", None), P(None, "blk", "pitch")),
        check_vma=False,
    )
```

```python
import functools

import jax
import jax.numpy as jnp
import numpy as np
from jax import lax
from jax.experimental import pallas as pl
from jax.experimental.pallas import tpu as pltpu
from jax.sharding import PartitionSpec as P

NH = 48
NV = 5
WV = 2 * NV
ROWS = 8
NU = 0.15
section_weights = (1.0 / 3.0, 0.5, 1.0)
MESH = pl.DeviceIdType.MESH
HIGHEST = lax.Precision.HIGHEST
NEAR = ((0, 1), (0, -1), (1, 0), (-1, 0))
RELAYS = (((0, 1, 0), (0, -1, 0), (0, 0, 1), (0, 0, -1)),
          ((-1, 0, 1), (-1, 1, 0), (-1, -1, 0), (1, 1, 0), (1, -1, 0)),
          ((2, 1, 0), (2, -1, 0)))


def harmonic_tables(slabs, slab):
    period = slabs * slab
    places = np.arange(period)[:, None]
    orders = np.arange(NH)[None, :]
    factor = np.where(orders == 0, 1.0, 2.0) / period
    cos_cols = np.cos(2.0 * np.pi * (places * orders % period) / period) * factor
    sin_cols = np.sin(2.0 * np.pi * (places * (orders + 1) % period) / period) * (2.0 / period)
    table = np.concatenate([cos_cols, sin_cols], 1)
    total = NV * 2 * NH
    chunk = total // slabs
    full = np.zeros((NV, period, total))
    for v in range(NV):
        full[v, :, v * 2 * NH:(v + 1) * 2 * NH] = table
    full = full.reshape(NV, slabs, slab, slabs, chunk).transpose(3, 1, 0, 2, 4)
    out = np.zeros((slabs, slabs, NV, slab, 128), np.float32)
    out[..., :chunk] = full
    return out


def kernel(blocks, slabs, speeds_hbm, blocks_hbm, states_hbm, steps_hbm, table_hbm, src_hbm, frac_hbm,
           out_ref, arr_ref,
           speeds, src_ref, frac_ref, q0, dt, table, partial, field, first, send, halo, inter, inter_b, inter_c,
           load_sem, send_sem, recv_sem, isend_sem, irecv_sem):
    b = lax.axis_index("blk")
    x = lax.axis_index("pitch")

    def device(db, dx):
        return {"blk": lax.rem(b + db + blocks, blocks), "pitch": lax.rem(x + dx + slabs, slabs)}

    barrier = pltpu.get_barrier_semaphore()

    def where_blocks(db, action):
        if db == 0:
            action()
        else:
            pl.when(b > 0 if db < 0 else b < blocks - 1)(action)

    def greet(db):
        for peer in NEAR:
            if peer[0] == db:
                pl.semaphore_signal(barrier, inc=1, device_id=device(*peer), device_id_type=MESH)
    for db in (0, -1, 1):
        where_blocks(db, functools.partial(greet, db))
    loads = [
        pltpu.make_async_copy(states_hbm, q0, load_sem.at[0]),
        pltpu.make_async_copy(steps_hbm, dt, load_sem.at[1]),
        pltpu.make_async_copy(table_hbm.at[x], table, load_sem.at[2]),
        pltpu.make_async_copy(speeds_hbm, speeds, load_sem.at[3]),
        pltpu.make_async_copy(src_hbm, src_ref, load_sem.at[4]),
        pltpu.make_async_copy(frac_hbm, frac_ref, load_sem.at[5]),
    ]
    for load in loads:
        load.start()

    lane = lax.broadcasted_iota(jnp.int32, (8, 128), 1)
    sub = lax.broadcasted_iota(jnp.int32, (8, 128), 0)

    @pl.when(b == 0)
    def _():
        for stage in range(3):
            halo[stage, 2] = jnp.zeros((WV, 8, 128), jnp.float32)
        inter[0] = jnp.zeros(inter.shape[1:], jnp.float32)

    @pl.when(b == blocks - 1)
    def _():
        for stage in range(3):
            halo[stage, 3] = jnp.zeros((WV, 8, 128), jnp.float32)
        inter[2] = jnp.zeros(inter.shape[1:], jnp.float32)

    def pack(source, stage, i):
        base = pl.multiple_of(i * 64, 64)
        send[stage, 0, i] = source[pl.ds(base + 7, 8, stride=8), :]
        send[stage, 1, i] = source[pl.ds(base, 8, stride=8), :]
        send[stage, 2, i] = source[pl.ds(base + 56, 8), :]
        send[stage, 3, i] = source[pl.ds(base, 8), :]

    faces = (first.at[0], first.at[1], blocks_hbm.at[:, ROWS - 1], blocks_hbm.at[:, 0])

    def exchange(stage):
        copies = []
        for d, (db, dx) in enumerate(NEAR):
            copies.append((db, pltpu.make_async_remote_copy(
                src_ref=faces[d] if stage == 0 else send.at[stage - 1, d], dst_ref=halo.at[stage, d],
                send_sem=send_sem.at[stage, d], recv_sem=recv_sem.at[stage, d],
                device_id=device(db, dx), device_id_type=MESH)))
        return copies

    def start(copies):
        for sign in (1, -1, 0):
            chosen = [copy for db, copy in copies if db == sign]
            if chosen:
                where_blocks(sign, lambda: [copy.start() for copy in chosen] and None)

    def wait_recv(copies):
        for sign in (0, 1, -1):
            chosen = [copy for db, copy in copies if db == sign]
            where_blocks(-sign, lambda: [copy.wait_recv() for copy in chosen] and None)

    def wait_send(copies):
        for sign in (0, 1, -1):
            chosen = [copy for db, copy in copies if db == sign]
            where_blocks(sign, lambda: [copy.wait_send() for copy in chosen] and None)

    below = (b + blocks - 1) // blocks
    above = (2 * blocks - 2 - b) // blocks
    pl.semaphore_wait(barrier, 2 + below + above)
    stages = [exchange(stage) for stage in range(3)]
    start([face for face in stages[0] if face[0] != 0])
    loads[0].wait()
    for i in range(WV):
        first[0, i] = q0[pl.ds(i * 64 + 7, 8, stride=8), :]
        first[1, i] = q0[pl.ds(i * 64, 8, stride=8), :]
    start([face for face in stages[0] if face[0] == 0])
    loads[1].wait()
    chosen = []
    for w in range(2):
        first = 124 if w == 0 else -4
        pick = jnp.where((sub // 4 == w) & (lane == sub + first), 1.0, 0.0)
        cells = jnp.concatenate([q0[w * 320:(w + 1) * 320, :], dt[w * 64:(w + 1) * 64, :]], 0)
        chosen.append(lax.dot_general(pick, cells, (((1,), (1,)), ((), ())),
                                      precision=HIGHEST, preferred_element_type=jnp.float32))
    packet = chosen[0] + chosen[1]
    for j in range(3):
        inter[1, x, j] = packet[:, j * 128:(j + 1) * 128]

    gathers = []
    for phase in RELAYS:
        copies = []
        for slab, db, dx in phase:
            k = sum(len(done) for done in gathers) + len(copies)
            at = lax.rem(x + slab + slabs, slabs)
            copies.append((db, pltpu.make_async_remote_copy(
                src_ref=inter.at[1, at], dst_ref=inter.at[1 - db, at],
                send_sem=isend_sem.at[k], recv_sem=irecv_sem.at[k],
                device_id=device(db, dx), device_id_type=MESH)))
        gathers.append(copies)
    start(gathers[0])

    def inner(source, weight):
        def update(w, v):
            base = pl.multiple_of((w * NV + v) * 64, 64)
            dbase = w * 64
            a0, a1, a2 = (speeds[k, w, v] for k in range(3))
            centre = -(a0 + a1 + a2) - 6.0 * NU
            axial_low = jnp.where(lane == 0, 0.0, a0 + NU)
            axial_high = jnp.where(lane == 127, 0.0, NU)
            pitch_low = jnp.where(sub == 0, 0.0, a2 + NU)
            pitch_high = jnp.where(sub == 7, 0.0, NU)
            rows = [source[pl.ds(base + r * 8, 8), :] for r in range(ROWS)]
            for r in range(ROWS):
                q = rows[r]
                total = centre * q
                total += axial_low * pltpu.roll(q, 1, 1)
                total += axial_high * pltpu.roll(q, 127, 1)
                total += pitch_low * pltpu.roll(q, 1, 0)
                total += pitch_high * pltpu.roll(q, 7, 0)
                if r > 0:
                    total += (a1 + NU) * rows[r - 1]
                if r < ROWS - 1:
                    total += NU * rows[r + 1]
                step = weight * dt[pl.ds(dbase + r * 8, 8), :]
                partial[pl.ds(base + r * 8, 8), :] = q0[pl.ds(base + r * 8, 8), :] + step * total

        def body(v, carry):
            for w in range(2):
                update(w, v)
            return carry
        lax.fori_loop(0, NV, body, 0)

    def outer(stage, target, weight):
        def update(w, v):
            i = w * NV + v
            base = pl.multiple_of(i * 64, 64)
            dbase = w * 64
            a1, a2 = (speeds[k, w, v] for k in range(1, 3))
            pitch_low = jnp.where(sub == 0, a2 + NU, 0.0)
            pitch_high = jnp.where(sub == 7, NU, 0.0)
            for r in range(ROWS):
                total = pitch_low * halo[stage, 0, i, pl.ds(r, 1), :]
                total += pitch_high * halo[stage, 1, i, pl.ds(r, 1), :]
                if r == 0:
                    total += (a1 + NU) * halo[stage, 2, i]
                if r == ROWS - 1:
                    total += NU * halo[stage, 3, i]
                step = weight * dt[pl.ds(dbase + r * 8, 8), :]
                target[pl.ds(base + r * 8, 8), :] = (
                    partial[pl.ds(base + r * 8, 8), :] + step * total)

        def body(v, carry):
            for w in range(2):
                update(w, v)
            if stage < 2:
                for w in range(2):
                    pack(target, stage, w * NV + v)
            return carry
        lax.fori_loop(0, NV, body, 0)

    def speed_lanes(k, j):
        def of(w, v):
            return speeds[k, w, v] if v < NV else 0.0
        return jnp.where(sub < 4,
                         jnp.where(lane < 64, of(0, 2 * j), of(0, 2 * j + 1)),
                         jnp.where(lane < 64, of(1, 2 * j), of(1, 2 * j + 1)))

    def interface_coefs():
        coefs = []
        for j in range(3):
            nu = NU if j < 2 else jnp.where(lane < 64, NU, 0.0)
            a0, a1, a2 = (speed_lanes(k, j) for k in range(3))
            coefs.append((-(a0 + a1 + a2) - 6.0 * nu,
                          jnp.where(sub == 4, 0.0, a0 + nu), jnp.where(sub == 3, 0.0, nu),
                          a1 + nu, nu, a2 + nu, nu))
        return coefs

    cell = lax.rem(lane, 8)
    row = lax.rem(lane, 64) // 8

    def interface_section(source, weight, coefs, s):
        before = lax.rem(s + slabs - 1, slabs)
        after = lax.rem(s + 1, slabs)
        result = []
        for d in range(3):
            last = inter[d, s, 2]
            step = weight * jnp.where(lane < 64, pltpu.roll(last, 64, 1), last)
            parts = []
            for j in range(3):
                c, xl, xh, rl, rh, pl_, ph = coefs[j]
                q = source[d, s, j]
                total = c * q + xl * pltpu.roll(q, 1, 0) + xh * pltpu.roll(q, 7, 0)
                total += pl_ * jnp.where(cell == 0, pltpu.roll(source[d, before, j], 121, 1),
                                         pltpu.roll(q, 1, 1))
                total += ph * jnp.where(cell == 7, pltpu.roll(source[d, after, j], 7, 1),
                                        pltpu.roll(q, 127, 1))
                low = pltpu.roll(q, 8, 1)
                if d > 0:
                    low = jnp.where(row == 0, pltpu.roll(source[d - 1, s, j], 72, 1), low)
                high = pltpu.roll(q, 120, 1)
                if d < 2:
                    high = jnp.where(row == 7, pltpu.roll(source[d + 1, s, j], 56, 1), high)
                total += rl * low + rh * high
                parts.append(inter[d, s, j] + step * total)
            result.append(parts)
        return result

    def interface_step(source, target, weight):
        def body(s, carry):
            coefs = interface_coefs()
            result = interface_section(source, weight, coefs, s)
            for d in range(3):
                for j in range(3):
                    target[d, s, j] = result[d][j]
            return carry
        lax.fori_loop(0, slabs, body, 0)

    def interface_last(source, weight):
        near = (lax.broadcasted_iota(jnp.int32, (8, 8), 0)
                == lax.broadcasted_iota(jnp.int32, (8, 8), 1))

        def column(ref, slot, w):
            line = jnp.broadcast_to(ref[slot, w:w + 1, :].astype(jnp.float32), (8, 8))
            return jnp.sum(jnp.where(near, line, 0.0), axis=1, keepdims=True)
        columns_of = [[(column(src_ref, slot, w), column(frac_ref, slot, w) * (1.0 / 65536.0))
                       for slot in range(3)] for w in range(2)]
        shares = []
        for w in range(2):
            per_block = []
            for d in range(3):
                place = ((b + d - 1) * ROWS + row).astype(jnp.float32)
                share = jnp.zeros((8, 128), jnp.float32)
                for origin, fraction in columns_of[w]:
                    share += jnp.where(origin == place, fraction, 0.0)
                per_block.append(share)
            shares.append(per_block)

        def body(s, total):
            coefs = interface_coefs()
            result = interface_section(source, weight, coefs, s)
            sides = []
            for w in range(2):
                at = 4 if w == 0 else 3
                columns = []
                for j in range(3):
                    columns.append(sum(jnp.broadcast_to(result[d][j][at:at + 1, :], (8, 128))
                                       * shares[w][d] for d in range(3)))
                sides.append(jnp.concatenate(columns, 1))
            lhs = jnp.concatenate(sides, 0)
            waves = []
            for v in range(NV):
                waves += [table[s, v]] * ROWS
            waves.append(jnp.zeros((64, 128), jnp.float32))
            rhs = jnp.concatenate(waves, 0)
            return total + jnp.dot(lhs, rhs, precision=HIGHEST,
                                   preferred_element_type=jnp.float32)
        total = lax.fori_loop(0, slabs, body, jnp.zeros((16, 128), jnp.float32))
        columns = arr_ref.shape[2]
        arr_ref[0] = total[0:8, 0:columns]
        arr_ref[1] = total[8:16, 0:columns]

    w1, w2, w3 = section_weights
    loads[3].wait()
    inner(q0, w1)
    wait_recv(gathers[0])
    start(gathers[1])
    wait_recv(stages[0])
    outer(0, field, w1)
    start(stages[1])

    inner(field, w2)
    wait_recv(gathers[1])
    start(gathers[2])
    wait_recv(stages[1])
    outer(1, field, w2)
    start(stages[2])

    inner(field, w3)
    wait_recv(gathers[2])
    interface_step(inter, inter_b, w1)
    interface_step(inter_b, inter_c, w2)
    for load in (loads[2], loads[4], loads[5]):
        load.wait()
    interface_last(inter_c, w3)
    for copies in gathers + stages[:2]:
        wait_send(copies)
    wait_recv(stages[2])
    outer(2, out_ref, w3)
    wait_send(stages[2])


def write_out(field_ref, arr_ref, field_hbm, arr_hbm, sems):
    quarter = field_ref.shape[0] // 4
    copies = [pltpu.make_async_copy(field_ref.at[pl.ds(k * quarter, quarter)],
                                    field_hbm.at[pl.ds(k * quarter, quarter)], sems.at[k])
              for k in range(4)]
    copies.append(pltpu.make_async_copy(arr_ref, arr_hbm, sems.at[4]))
    for copy in copies:
        copy.start()
    for copy in copies:
        copy.wait()


def shards(tables, states, time_steps, speeds, band_src, band_frac):
    blocks = lax.axis_size("blk")
    slabs = lax.axis_size("pitch")
    any_space = pl.BlockSpec(memory_space=pl.ANY)
    vmem = pl.BlockSpec(memory_space=pltpu.VMEM)
    cells = WV * ROWS * 8
    columns = NV * 2 * NH // slabs
    field, arrivals = pl.pallas_call(
        functools.partial(kernel, blocks, slabs),
        out_shape=(pltpu.VMEM((cells, 128), jnp.float32),
                   pltpu.VMEM((2, ROWS, columns), jnp.float32)),
        in_specs=[any_space] * 7,
        out_specs=(vmem, vmem),
        scratch_shapes=[
            pltpu.SMEM((3, 2, NV), jnp.float32),
            pltpu.VMEM((3, 2, ROWS), jnp.int32),
            pltpu.VMEM((3, 2, ROWS), jnp.int32),
            pltpu.VMEM((cells, 128), jnp.float32),
            pltpu.VMEM((128, 128), jnp.float32),
            pltpu.VMEM((slabs, NV, 8, 128), jnp.float32),
            pltpu.VMEM((cells, 128), jnp.float32),
            pltpu.VMEM((cells, 128), jnp.float32),
            pltpu.VMEM((2, WV, 8, 128), jnp.float32),
            pltpu.VMEM((2, 4, WV, 8, 128), jnp.float32),
            pltpu.VMEM((3, 4, WV, 8, 128), jnp.float32),
            pltpu.VMEM((3, slabs, 3, 8, 128), jnp.float32),
            pltpu.VMEM((3, slabs, 3, 8, 128), jnp.float32),
            pltpu.VMEM((3, slabs, 3, 8, 128), jnp.float32),
            pltpu.SemaphoreType.DMA((6,)),
            pltpu.SemaphoreType.DMA((3, 4)),
            pltpu.SemaphoreType.DMA((3, 4)),
            pltpu.SemaphoreType.DMA((sum(len(phase) for phase in RELAYS),)),
            pltpu.SemaphoreType.DMA((sum(len(phase) for phase in RELAYS),)),
        ],
        compiler_params=pltpu.CompilerParams(collective_id=0, has_side_effects=True),
        name="window",
    )(jnp.transpose(speeds, (2, 0, 1)), states.reshape(WV, ROWS, 8, 128),
      states.reshape(cells, 128), time_steps.reshape(128, 128),
      jnp.asarray(tables), jnp.transpose(band_src, (2, 0, 1)), jnp.transpose(band_frac, (2, 0, 1)))
    field, arrivals = pl.pallas_call(
        write_out,
        out_shape=(jax.ShapeDtypeStruct(field.shape, jnp.float32),
                   jax.ShapeDtypeStruct(arrivals.shape, jnp.float32)),
        in_specs=[vmem] * 2,
        out_specs=(any_space, any_space),
        scratch_shapes=[pltpu.SemaphoreType.DMA((5,))],
        name="write_out",
    )(pltpu.with_memory_space_constraint(field, pltpu.VMEM),
      pltpu.with_memory_space_constraint(arrivals, pltpu.VMEM))
    return field.reshape(states.shape), arrivals


def solution(mesh):
    tables = harmonic_tables(mesh.shape["pitch"], 8)
    return jax.shard_map(
        functools.partial(shards, tables),
        mesh=mesh,
        in_specs=(
            P(None, None, "blk", "pitch", None),
            P(None, "blk", "pitch", None),
            P(),
            P(None, "blk", None),
            P(None, "blk", None),
        ),
        out_specs=(P(None, None, "blk", "pitch", None), P(None, "blk", "pitch")),
        check_vma=False,
    )
```

```python
import functools

import jax
import jax.numpy as jnp
import numpy as np
from jax import lax
from jax.experimental import pallas as pl
from jax.experimental.pallas import tpu as pltpu
from jax.sharding import PartitionSpec as P

NH = 48
NV = 5
WV = 2 * NV
ROWS = 8
NU = 0.15
section_weights = (1.0 / 3.0, 0.5, 1.0)
MESH = pl.DeviceIdType.MESH
HIGHEST = lax.Precision.HIGHEST
NEAR = ((0, 1), (0, -1), (1, 0), (-1, 0))
RELAYS = (((0, 1, 0), (0, -1, 0), (0, 0, 1), (0, 0, -1)),
          ((-1, 0, 1), (-1, 1, 0), (-1, -1, 0), (1, 1, 0), (1, -1, 0)),
          ((2, 1, 0), (2, -1, 0)))


def harmonic_tables(slabs, slab):
    period = slabs * slab
    places = np.arange(period)[:, None]
    orders = np.arange(NH)[None, :]
    factor = np.where(orders == 0, 1.0, 2.0) / period
    cos_cols = np.cos(2.0 * np.pi * (places * orders % period) / period) * factor
    sin_cols = np.sin(2.0 * np.pi * (places * (orders + 1) % period) / period) * (2.0 / period)
    table = np.concatenate([cos_cols, sin_cols], 1)
    total = NV * 2 * NH
    chunk = total // slabs
    full = np.zeros((NV, period, total))
    for v in range(NV):
        full[v, :, v * 2 * NH:(v + 1) * 2 * NH] = table
    full = full.reshape(NV, slabs, slab, slabs, chunk).transpose(3, 1, 0, 2, 4)
    out = np.zeros((slabs, slabs, NV, slab, 128), np.float32)
    out[..., :chunk] = full
    return out


def kernel(blocks, slabs, speeds_hbm, blocks_hbm, states_hbm, steps_hbm, table_hbm, src_hbm, frac_hbm,
           out_ref, arr_ref,
           speeds, src_ref, frac_ref, q0, dt, table, partial, field, first, send, halo, inter, inter_b, inter_c,
           load_sem, send_sem, recv_sem, isend_sem, irecv_sem):
    b = lax.axis_index("blk")
    x = lax.axis_index("pitch")

    def device(db, dx):
        return {"blk": lax.rem(b + db + blocks, blocks), "pitch": lax.rem(x + dx + slabs, slabs)}

    barrier = pltpu.get_barrier_semaphore()

    def where_blocks(db, action):
        if db == 0:
            action()
        else:
            pl.when(b > 0 if db < 0 else b < blocks - 1)(action)

    def greet(db):
        for peer in NEAR:
            if peer[0] == db:
                pl.semaphore_signal(barrier, inc=1, device_id=device(*peer), device_id_type=MESH)
    for db in (0, -1, 1):
        where_blocks(db, functools.partial(greet, db))
    loads = [
        pltpu.make_async_copy(states_hbm, q0, load_sem.at[0]),
        pltpu.make_async_copy(steps_hbm, dt, load_sem.at[1]),
        pltpu.make_async_copy(table_hbm.at[x], table, load_sem.at[2]),
        pltpu.make_async_copy(speeds_hbm, speeds, load_sem.at[3]),
        pltpu.make_async_copy(src_hbm, src_ref, load_sem.at[4]),
        pltpu.make_async_copy(frac_hbm, frac_ref, load_sem.at[5]),
    ]
    for load in loads:
        load.start()

    lane = lax.broadcasted_iota(jnp.int32, (8, 128), 1)
    sub = lax.broadcasted_iota(jnp.int32, (8, 128), 0)

    @pl.when(b == 0)
    def _():
        for stage in range(3):
            halo[stage, 2] = jnp.zeros((WV, 8, 128), jnp.float32)
        inter[0] = jnp.zeros(inter.shape[1:], jnp.float32)

    @pl.when(b == blocks - 1)
    def _():
        for stage in range(3):
            halo[stage, 3] = jnp.zeros((WV, 8, 128), jnp.float32)
        inter[2] = jnp.zeros(inter.shape[1:], jnp.float32)

    faces = (first.at[0], first.at[1], blocks_hbm.at[:, ROWS - 1], blocks_hbm.at[:, 0])

    def exchange(stage):
        copies = []
        for d, (db, dx) in enumerate(NEAR):
            copies.append((db, pltpu.make_async_remote_copy(
                src_ref=faces[d] if stage == 0 else send.at[stage - 1, d], dst_ref=halo.at[stage, d],
                send_sem=send_sem.at[stage, d], recv_sem=recv_sem.at[stage, d],
                device_id=device(db, dx), device_id_type=MESH)))
        return copies

    def start(copies):
        for sign in (1, -1, 0):
            chosen = [copy for db, copy in copies if db == sign]
            if chosen:
                where_blocks(sign, lambda: [copy.start() for copy in chosen] and None)

    def wait_recv(copies):
        for sign in (0, 1, -1):
            chosen = [copy for db, copy in copies if db == sign]
            if chosen:
                where_blocks(-sign, lambda: [copy.wait_recv() for copy in chosen] and None)

    def wait_send(copies):
        for sign in (0, 1, -1):
            chosen = [copy for db, copy in copies if db == sign]
            where_blocks(sign, lambda: [copy.wait_send() for copy in chosen] and None)

    below = (b + blocks - 1) // blocks
    above = (2 * blocks - 2 - b) // blocks
    pl.semaphore_wait(barrier, 2 + below + above)
    stages = [exchange(stage) for stage in range(3)]
    start([face for face in stages[0] if face[0] != 0])
    loads[0].wait()
    for i in range(WV):
        first[0, i] = q0[pl.ds(i * 64 + 7, 8, stride=8), :]
        first[1, i] = q0[pl.ds(i * 64, 8, stride=8), :]
    start([face for face in stages[0] if face[0] == 0])
    loads[1].wait()
    chosen = []
    for w in range(2):
        first = 124 if w == 0 else -4
        pick = jnp.where((sub // 4 == w) & (lane == sub + first), 1.0, 0.0)
        cells = jnp.concatenate([q0[w * 320:(w + 1) * 320, :], dt[w * 64:(w + 1) * 64, :]], 0)
        chosen.append(lax.dot_general(pick, cells, (((1,), (1,)), ((), ())),
                                      precision=HIGHEST, preferred_element_type=jnp.float32))
    packet = chosen[0] + chosen[1]
    for j in range(3):
        inter[1, x, j] = packet[:, j * 128:(j + 1) * 128]

    gathers = []
    for phase in RELAYS:
        copies = []
        for slab, db, dx in phase:
            k = sum(len(done) for done in gathers) + len(copies)
            at = lax.rem(x + slab + slabs, slabs)
            copies.append((db, pltpu.make_async_remote_copy(
                src_ref=inter.at[1, at], dst_ref=inter.at[1 - db, at],
                send_sem=isend_sem.at[k], recv_sem=irecv_sem.at[k],
                device_id=device(db, dx), device_id_type=MESH)))
        gathers.append(copies)
    start(gathers[0])

    def inner(source, weight):
        def update(w, v):
            base = pl.multiple_of((w * NV + v) * 64, 64)
            dbase = w * 64
            a0, a1, a2 = (speeds[k, w, v] for k in range(3))
            centre = -(a0 + a1 + a2) - 6.0 * NU
            axial_low = jnp.where(lane == 0, 0.0, a0 + NU)
            axial_high = jnp.where(lane == 127, 0.0, NU)
            pitch_low = jnp.where(sub == 0, 0.0, a2 + NU)
            pitch_high = jnp.where(sub == 7, 0.0, NU)
            rows = [source[pl.ds(base + r * 8, 8), :] for r in range(ROWS)]
            for r in range(ROWS):
                q = rows[r]
                total = centre * q
                total += axial_low * pltpu.roll(q, 1, 1)
                total += axial_high * pltpu.roll(q, 127, 1)
                total += pitch_low * pltpu.roll(q, 1, 0)
                total += pitch_high * pltpu.roll(q, 7, 0)
                if r > 0:
                    total += (a1 + NU) * rows[r - 1]
                if r < ROWS - 1:
                    total += NU * rows[r + 1]
                step = weight * dt[pl.ds(dbase + r * 8, 8), :]
                partial[pl.ds(base + r * 8, 8), :] = q0[pl.ds(base + r * 8, 8), :] + step * total

        def body(v, carry):
            for w in range(2):
                update(w, v)
            return carry
        lax.fori_loop(0, NV, body, 0)

    def outer_pitch(stage, target, weight):
        def update(w, v):
            i = w * NV + v
            base = pl.multiple_of(i * 64, 64)
            dbase = w * 64
            a2 = speeds[2, w, v]
            pitch_low = jnp.where(sub == 0, a2 + NU, 0.0)
            pitch_high = jnp.where(sub == 7, NU, 0.0)
            for r in range(ROWS):
                total = pitch_low * halo[stage, 0, i, pl.ds(r, 1), :]
                total += pitch_high * halo[stage, 1, i, pl.ds(r, 1), :]
                step = weight * dt[pl.ds(dbase + r * 8, 8), :]
                target[pl.ds(base + r * 8, 8), :] = (
                    partial[pl.ds(base + r * 8, 8), :] + step * total)

        def body(v, carry):
            for w in range(2):
                update(w, v)
            return carry
        lax.fori_loop(0, NV, body, 0)

    def outer_radial(stage, target, weight):
        def body(v, carry):
            for w in range(2):
                i = w * NV + v
                a1 = speeds[1, w, v]
                for r, side, factor in ((ROWS - 1, 3, NU), (0, 2, a1 + NU)):
                    place = pl.ds(pl.multiple_of(i * 64, 64) + r * 8, 8)
                    step = weight * dt[w * 64 + r * 8:w * 64 + r * 8 + 8, :]
                    value = target[place, :] + (step * factor) * halo[stage, side, i]
                    target[place, :] = value
                    if stage < 2:
                        send[stage, 2 if r else 3, i] = value
            return carry
        lax.fori_loop(0, NV, body, 0)

    def pack_pitch(stage, source):
        def body(v, carry):
            for w in range(2):
                i = w * NV + v
                base = pl.multiple_of(i * 64, 64)
                send[stage, 0, i] = source[pl.ds(base + 7, 8, stride=8), :]
                send[stage, 1, i] = source[pl.ds(base, 8, stride=8), :]
            return carry
        lax.fori_loop(0, NV, body, 0)

    def pitch_of(copies):
        return [copy for copy in copies if copy[0] == 0]

    def radial_of(copies):
        return [copy for copy in copies if copy[0] != 0]

    def arrive(stage, target, weight):
        wait_recv(pitch_of(stages[stage]))
        outer_pitch(stage, target, weight)
        wait_recv(radial_of(stages[stage]))
        outer_radial(stage, target, weight)
        if stage < 2:
            start(radial_of(stages[stage + 1]))
            pack_pitch(stage, target)
            start(pitch_of(stages[stage + 1]))

    def speed_lanes(k, j):
        def of(w, v):
            return speeds[k, w, v] if v < NV else 0.0
        return jnp.where(sub < 4,
                         jnp.where(lane < 64, of(0, 2 * j), of(0, 2 * j + 1)),
                         jnp.where(lane < 64, of(1, 2 * j), of(1, 2 * j + 1)))

    def interface_coefs():
        coefs = []
        for j in range(3):
            nu = NU if j < 2 else jnp.where(lane < 64, NU, 0.0)
            a0, a1, a2 = (speed_lanes(k, j) for k in range(3))
            coefs.append((-(a0 + a1 + a2) - 6.0 * nu,
                          jnp.where(sub == 4, 0.0, a0 + nu), jnp.where(sub == 3, 0.0, nu),
                          a1 + nu, nu, a2 + nu, nu))
        return coefs

    cell = lax.rem(lane, 8)
    row = lax.rem(lane, 64) // 8

    def interface_section(source, weight, coefs, s):
        before = lax.rem(s + slabs - 1, slabs)
        after = lax.rem(s + 1, slabs)
        result = []
        for d in range(3):
            last = inter[d, s, 2]
            step = weight * jnp.where(lane < 64, pltpu.roll(last, 64, 1), last)
            parts = []
            for j in range(3):
                c, xl, xh, rl, rh, pl_, ph = coefs[j]
                q = source[d, s, j]
                total = c * q + xl * pltpu.roll(q, 1, 0) + xh * pltpu.roll(q, 7, 0)
                total += pl_ * jnp.where(cell == 0, pltpu.roll(source[d, before, j], 121, 1),
                                         pltpu.roll(q, 1, 1))
                total += ph * jnp.where(cell == 7, pltpu.roll(source[d, after, j], 7, 1),
                                        pltpu.roll(q, 127, 1))
                low = pltpu.roll(q, 8, 1)
                if d > 0:
                    low = jnp.where(row == 0, pltpu.roll(source[d - 1, s, j], 72, 1), low)
                high = pltpu.roll(q, 120, 1)
                if d < 2:
                    high = jnp.where(row == 7, pltpu.roll(source[d + 1, s, j], 56, 1), high)
                total += rl * low + rh * high
                parts.append(inter[d, s, j] + step * total)
            result.append(parts)
        return result

    def interface_step(source, target, weight):
        def body(s, carry):
            coefs = interface_coefs()
            result = interface_section(source, weight, coefs, s)
            for d in range(3):
                for j in range(3):
                    target[d, s, j] = result[d][j]
            return carry
        lax.fori_loop(0, slabs, body, 0)

    def interface_last(source, weight):
        near = (lax.broadcasted_iota(jnp.int32, (8, 8), 0)
                == lax.broadcasted_iota(jnp.int32, (8, 8), 1))

        def column(ref, slot, w):
            line = jnp.broadcast_to(ref[slot, w:w + 1, :].astype(jnp.float32), (8, 8))
            return jnp.sum(jnp.where(near, line, 0.0), axis=1, keepdims=True)
        columns_of = [[(column(src_ref, slot, w), column(frac_ref, slot, w) * (1.0 / 65536.0))
                       for slot in range(3)] for w in range(2)]
        shares = []
        for w in range(2):
            per_block = []
            for d in range(3):
                place = ((b + d - 1) * ROWS + row).astype(jnp.float32)
                share = jnp.zeros((8, 128), jnp.float32)
                for origin, fraction in columns_of[w]:
                    share += jnp.where(origin == place, fraction, 0.0)
                per_block.append(share)
            shares.append(per_block)

        def body(s, total):
            coefs = interface_coefs()
            result = interface_section(source, weight, coefs, s)
            sides = []
            for w in range(2):
                at = 4 if w == 0 else 3
                columns = []
                for j in range(3):
                    columns.append(sum(jnp.broadcast_to(result[d][j][at:at + 1, :], (8, 128))
                                       * shares[w][d] for d in range(3)))
                sides.append(jnp.concatenate(columns, 1))
            lhs = jnp.concatenate(sides, 0)
            waves = []
            for v in range(NV):
                waves += [table[s, v]] * ROWS
            waves.append(jnp.zeros((64, 128), jnp.float32))
            rhs = jnp.concatenate(waves, 0)
            return total + jnp.dot(lhs, rhs, precision=HIGHEST,
                                   preferred_element_type=jnp.float32)
        total = lax.fori_loop(0, slabs, body, jnp.zeros((16, 128), jnp.float32))
        columns = arr_ref.shape[2]
        arr_ref[0] = total[0:8, 0:columns]
        arr_ref[1] = total[8:16, 0:columns]

    w1, w2, w3 = section_weights
    loads[3].wait()
    inner(q0, w1)
    wait_recv(gathers[0])
    start(gathers[1])
    arrive(0, field, w1)

    inner(field, w2)
    wait_recv(gathers[1])
    start(gathers[2])
    arrive(1, field, w2)

    inner(field, w3)
    wait_recv(gathers[2])
    interface_step(inter, inter_b, w1)
    interface_step(inter_b, inter_c, w2)
    for load in (loads[2], loads[4], loads[5]):
        load.wait()
    interface_last(inter_c, w3)
    for copies in gathers + stages[:2]:
        wait_send(copies)
    arrive(2, out_ref, w3)
    wait_send(stages[2])


def write_out(field_ref, arr_ref, field_hbm, arr_hbm, sems):
    quarter = field_ref.shape[0] // 4
    copies = [pltpu.make_async_copy(field_ref.at[pl.ds(k * quarter, quarter)],
                                    field_hbm.at[pl.ds(k * quarter, quarter)], sems.at[k])
              for k in range(4)]
    copies.append(pltpu.make_async_copy(arr_ref, arr_hbm, sems.at[4]))
    for copy in copies:
        copy.start()
    for copy in copies:
        copy.wait()


def shards(tables, states, time_steps, speeds, band_src, band_frac):
    blocks = lax.axis_size("blk")
    slabs = lax.axis_size("pitch")
    any_space = pl.BlockSpec(memory_space=pl.ANY)
    vmem = pl.BlockSpec(memory_space=pltpu.VMEM)
    cells = WV * ROWS * 8
    columns = NV * 2 * NH // slabs
    field, arrivals = pl.pallas_call(
        functools.partial(kernel, blocks, slabs),
        out_shape=(pltpu.VMEM((cells, 128), jnp.float32),
                   pltpu.VMEM((2, ROWS, columns), jnp.float32)),
        in_specs=[any_space] * 7,
        out_specs=(vmem, vmem),
        scratch_shapes=[
            pltpu.SMEM((3, 2, NV), jnp.float32),
            pltpu.VMEM((3, 2, ROWS), jnp.int32),
            pltpu.VMEM((3, 2, ROWS), jnp.int32),
            pltpu.VMEM((cells, 128), jnp.float32),
            pltpu.VMEM((128, 128), jnp.float32),
            pltpu.VMEM((slabs, NV, 8, 128), jnp.float32),
            pltpu.VMEM((cells, 128), jnp.float32),
            pltpu.VMEM((cells, 128), jnp.float32),
            pltpu.VMEM((2, WV, 8, 128), jnp.float32),
            pltpu.VMEM((2, 4, WV, 8, 128), jnp.float32),
            pltpu.VMEM((3, 4, WV, 8, 128), jnp.float32),
            pltpu.VMEM((3, slabs, 3, 8, 128), jnp.float32),
            pltpu.VMEM((3, slabs, 3, 8, 128), jnp.float32),
            pltpu.VMEM((3, slabs, 3, 8, 128), jnp.float32),
            pltpu.SemaphoreType.DMA((6,)),
            pltpu.SemaphoreType.DMA((3, 4)),
            pltpu.SemaphoreType.DMA((3, 4)),
            pltpu.SemaphoreType.DMA((sum(len(phase) for phase in RELAYS),)),
            pltpu.SemaphoreType.DMA((sum(len(phase) for phase in RELAYS),)),
        ],
        compiler_params=pltpu.CompilerParams(collective_id=0, has_side_effects=True),
        name="window",
    )(jnp.transpose(speeds, (2, 0, 1)), states.reshape(WV, ROWS, 8, 128),
      states.reshape(cells, 128), time_steps.reshape(128, 128),
      jnp.asarray(tables), jnp.transpose(band_src, (2, 0, 1)), jnp.transpose(band_frac, (2, 0, 1)))
    field, arrivals = pl.pallas_call(
        write_out,
        out_shape=(jax.ShapeDtypeStruct(field.shape, jnp.float32),
                   jax.ShapeDtypeStruct(arrivals.shape, jnp.float32)),
        in_specs=[vmem] * 2,
        out_specs=(any_space, any_space),
        scratch_shapes=[pltpu.SemaphoreType.DMA((5,))],
        name="write_out",
    )(pltpu.with_memory_space_constraint(field, pltpu.VMEM),
      pltpu.with_memory_space_constraint(arrivals, pltpu.VMEM))
    return field.reshape(states.shape), arrivals


def solution(mesh):
    tables = harmonic_tables(mesh.shape["pitch"], 8)
    return jax.shard_map(
        functools.partial(shards, tables),
        mesh=mesh,
        in_specs=(
            P(None, None, "blk", "pitch", None),
            P(None, "blk", "pitch", None),
            P(),
            P(None, "blk", None),
            P(None, "blk", None),
        ),
        out_specs=(P(None, None, "blk", "pitch", None), P(None, "blk", "pitch")),
        check_vma=False,
    )
```
